512 devices in a mesh: uly: 8 (over x, z_lo), blk: 64 (over y, z_hi, core).
Axes of the slice: x: 4, y: 8, z: 8 (z_hi: 4, z_lo: 2; z = z_hi * 2 + z_lo), core: 2. Of those that a mesh axis runs over, the one named last changes fastest.
Arguments:
- prompt: bfloat16 [64, 128, 3072], P('blk')
- image_rows: bfloat16 [8, 64, 8, 3072], P('uly', 'blk'), may hold values from -6 to 6
- image_slots: int32 [8, 64, 8], P('uly', 'blk'), may hold values from -1 to 127, as said below
- norm_gain: float32 [3072], replicated, may hold values from 0.1 to 1.9
- w_query: bfloat16 [3072, 3072], P(None, 'uly')
- key_matrix: bfloat16 [3072, 1024], P(None, 'uly'), may hold values from -0.109375 to 0.109375
- value_matrix: bfloat16 [3072, 1024], P(None, 'uly'), may hold values from -0.109375 to 0.109375
- w_out: bfloat16 [3072, 3072], P('uly', 'blk'), may hold values from -0.109375 to 0.109375
Outputs:
- hidden_out: bfloat16 [64, 128, 3072], P('blk', 'uly')
The draws below stay inside these ranges and needn't reach their ends.
Inputs may be any that keep to these rules, and one draw needn't show every extreme that they name: `image_slots`: entry (u, b, s) is -1 for an empty slot or a position inside block b. The live entries of one block are distinct and form one run of consecutive positions, of 8 up to three times 8 image rows, held by one to three devices of that block; in every block one device holds exactly 8 live rows.
All inputs are finite; a program needn't handle non-finite values.
Results may differ from the reference program's by a relative error of at most 0.0075.
The reference program's roundings to bfloat16 on the way count: a program that leaves them out, or rounds other values in their place, can miss the bound.
Values may be sent and summed in bfloat16 or wider, within the bound.
No kernel may reach another device: no remote copies, remote signals or barrier semaphores. Data moves between devices by JAX's collectives and lax.ppermute only.
A program may use at most 64 MiB of HBM per device.

```python
import math
import jax
import jax.numpy as jnp
from jax import lax

MODEL_WIDTH = 3072
QUERY_HEADS = 24
KEY_VALUE_HEADS = 8
HEAD_SIZE = 128
IMG_DEV = 8
BLOCK_POSITIONS = 128
SEQUENCE_LENGTH = 8192
N_ULY = 8
N_BLK = 64


def draw_prompt(key, part):
    streams = jax.random.split(key, 3)
    base = jax.random.normal(streams[0], (N_BLK, BLOCK_POSITIONS, MODEL_WIDTH), jnp.float32)
    row_scale = jnp.exp(jax.random.uniform(streams[1], (N_BLK, BLOCK_POSITIONS, 1), jnp.float32, math.log(0.3), math.log(3.0)))
    column_scale = jnp.exp(jax.random.uniform(streams[2], (1, 1, MODEL_WIDTH), jnp.float32, math.log(0.3), math.log(3.0)))
    return (base * row_scale * column_scale).astype(jnp.bfloat16)


def draw_w_query(key, part):
    factor = 3.0 / math.sqrt(MODEL_WIDTH)
    return (jax.random.normal(key, (MODEL_WIDTH, QUERY_HEADS * HEAD_SIZE), jnp.float32) * factor).astype(jnp.bfloat16)


def draw_image_slots(key, part):
    streams = jax.random.split(key, 3)
    longest = min(3, N_ULY) * IMG_DEV
    lengths = jax.random.randint(streams[0], (N_BLK,), IMG_DEV, longest + 1)
    starts = jax.random.randint(streams[1], (N_BLK,), 0, BLOCK_POSITIONS - lengths + 1)
    first_owner = jax.random.randint(streams[2], (N_BLK,), 0, N_ULY)
    owner = jnp.arange(N_ULY, dtype=jnp.int32)[:, None, None]
    slot_index = jnp.arange(IMG_DEV, dtype=jnp.int32)[None, None, :]
    offset = (owner - first_owner[None, :, None]) % N_ULY * IMG_DEV + slot_index
    live = offset < lengths[None, :, None]
    return jnp.where(live, starts[None, :, None] + offset, -1).astype(jnp.int32)


def levels(rng, shape, cuts, smallest, high):
    def one(axis_at, blocks):
        heights = jax.random.uniform(jax.random.fold_in(jax.random.fold_in(rng, 6), axis_at), (blocks,), jnp.float32, smallest / len(cuts), high / len(cuts))
        return jnp.repeat(jnp.exp(heights), shape[axis_at] // blocks).reshape((-1,) + (1,) * (len(shape) - axis_at - 1))

    gain = one(*cuts[0])
    for cut in cuts[1:]:
        gain = gain * one(*cut)
    return gain


def centred(rng, extent, width, bound, cuts=(), held_as=jnp.bfloat16):
    entries = jax.random.normal(rng, extent, jnp.float32) * width
    if len(cuts) > 0:
        entries = levels(rng, extent, cuts, -0.22, 0.18) * entries
    return jnp.clip(entries, min=-bound, max=bound).astype(held_as)


def setup_inputs(seed: int = 0) -> dict:
    key_of = jax.random.split(jax.random.key(seed), 9)
    prompt = draw_prompt(jax.random.fold_in(key_of[8], 71), 0)
    image_rows = centred(key_of[1], (N_ULY, N_BLK, IMG_DEV, MODEL_WIDTH), 1.0, 6.0, ((0, 8), (1, 64)))
    image_slots = draw_image_slots(jax.random.fold_in(key_of[8], 71), 0)
    norm_gain = jnp.clip(1.0 + 0.18 * jax.random.normal(key_of[3], (MODEL_WIDTH,), jnp.float32), 0.1, 1.9)
    w_query = draw_w_query(jax.random.fold_in(key_of[8], 71), 0)
    key_matrix = centred(key_of[5], (MODEL_WIDTH, KEY_VALUE_HEADS * HEAD_SIZE), MODEL_WIDTH ** -0.5, 0.109375, ((1, 8),))
    value_matrix = centred(key_of[6], (MODEL_WIDTH, KEY_VALUE_HEADS * HEAD_SIZE), MODEL_WIDTH ** -0.5, 0.109375, ((1, 8),))
    w_out = centred(key_of[7], (QUERY_HEADS * HEAD_SIZE, MODEL_WIDTH), (QUERY_HEADS * HEAD_SIZE) ** -0.5, 0.109375, ((0, 8), (1, 64)))
    return {"prompt": prompt, "image_rows": image_rows, "image_slots": image_slots, "norm_gain": norm_gain, "w_query": w_query, "key_matrix": key_matrix, "value_matrix": value_matrix, "w_out": w_out}


def rope_tables(positions, head_width):
    fraction = jnp.arange(0, head_width, 2).astype(jnp.float32) / head_width
    inverse = jnp.exp(-math.log(500000.0) * fraction)
    angles = positions.astype(jnp.float32)[:, None] * inverse[None, :]
    angles = jnp.concatenate([angles, angles], axis=1)
    return (jnp.cos(angles), jnp.sin(angles))

def rotate_halves(values, cosine_table, sine_table):
    half_width = values.shape[-1] // 2
    turned = jnp.concatenate([-values[..., half_width:], values[..., :half_width]], axis=-1)
    return values * cosine_table + turned * sine_table

def reference(prompt, image_rows, image_slots, norm_gain, w_query, key_matrix, value_matrix, w_out):
    group_count = QUERY_HEADS // KEY_VALUE_HEADS
    picture_embedding_vectors = jnp.transpose(image_rows, (1, 0, 2, 3)).reshape(N_BLK, N_ULY * IMG_DEV, MODEL_WIDTH).astype(jnp.float32)
    placeholder_labels = jnp.transpose(image_slots, (1, 0, 2)).reshape(N_BLK, N_ULY * IMG_DEV)
    equality_flags = placeholder_labels[:, None, :] == jnp.arange(BLOCK_POSITIONS, dtype=jnp.int32)[None, :, None]
    chosen_entries = jnp.einsum('ayl,alm->aym', equality_flags.astype(jnp.float32), picture_embedding_vectors)
    placed = jnp.where(jnp.any(equality_flags, axis=2)[:, :, None], chosen_entries, prompt.astype(jnp.float32)).reshape(SEQUENCE_LENGTH, MODEL_WIDTH)
    mean_square = lax.optimization_barrier(jnp.mean(placed * placed, axis=1, keepdims=True))
    normed_input = (placed * lax.rsqrt(mean_square + 1e-05) * norm_gain[None, :]).astype(jnp.bfloat16)
    positions = jnp.arange(SEQUENCE_LENGTH, dtype=jnp.int32)
    cosine_table, sine_table = rope_tables(positions, HEAD_SIZE)
    cosine_table = cosine_table[:, None, :]
    sine_table = sine_table[:, None, :]
    query_rows = jnp.dot(normed_input, w_query, preferred_element_type=jnp.float32).reshape(SEQUENCE_LENGTH, QUERY_HEADS, HEAD_SIZE)
    query_rows = rotate_halves(query_rows, cosine_table, sine_table).astype(jnp.bfloat16).reshape(SEQUENCE_LENGTH, KEY_VALUE_HEADS, group_count, HEAD_SIZE)
    key = jnp.dot(normed_input, key_matrix, preferred_element_type=jnp.float32).reshape(SEQUENCE_LENGTH, KEY_VALUE_HEADS, HEAD_SIZE)
    key = rotate_halves(key, cosine_table, sine_table).astype(jnp.bfloat16)
    value_rows = jnp.dot(normed_input, value_matrix, preferred_element_type=jnp.float32).astype(jnp.bfloat16).reshape(SEQUENCE_LENGTH, KEY_VALUE_HEADS, HEAD_SIZE)
    scale = 1.0 / math.sqrt(HEAD_SIZE)

    def attend_causal(position_index):
        block_number = position_index // KEY_VALUE_HEADS
        head_number = position_index % KEY_VALUE_HEADS
        queries = lax.dynamic_slice_in_dim(query_rows, (block_number * BLOCK_POSITIONS).astype(jnp.int32), BLOCK_POSITIONS, 0)
        queries = lax.dynamic_index_in_dim(queries, head_number, 1, keepdims=False).astype(jnp.float32)
        keys = lax.dynamic_index_in_dim(key, head_number, 1, keepdims=False).astype(jnp.float32)
        values = lax.dynamic_index_in_dim(value_rows, head_number, 1, keepdims=False).astype(jnp.float32)
        scores = jnp.einsum('qrd,sd->rqs', queries, keys) * scale
        query_pos = block_number * BLOCK_POSITIONS + jnp.arange(BLOCK_POSITIONS, dtype=jnp.int32)
        allowed = jnp.arange(SEQUENCE_LENGTH, dtype=jnp.int32)[None, :] <= query_pos[:, None]
        scores = jnp.where(allowed[None], scores, -jnp.inf)
        top_score = lax.optimization_barrier(jnp.max(scores, axis=2, keepdims=True))
        weights = jnp.exp(scores - top_score)
        total = lax.optimization_barrier(jnp.sum(weights, axis=2, keepdims=True))
        mixed = jnp.einsum('rqs,sd->rqd', weights.astype(jnp.bfloat16).astype(jnp.float32), values)
        return (mixed / total).astype(jnp.bfloat16)
    head_outputs = lax.map(attend_causal, jnp.arange(N_BLK * KEY_VALUE_HEADS, dtype=jnp.int32))
    head_outputs = head_outputs.reshape(N_BLK, KEY_VALUE_HEADS, group_count, BLOCK_POSITIONS, HEAD_SIZE)
    attended = jnp.transpose(head_outputs, (0, 3, 1, 2, 4)).reshape(SEQUENCE_LENGTH, QUERY_HEADS * HEAD_SIZE)
    projected = jnp.dot(attended, w_out, preferred_element_type=jnp.float32)
    return (placed + projected).astype(jnp.bfloat16).reshape(N_BLK, BLOCK_POSITIONS, MODEL_WIDTH)
```

```python
import functools
import math

import jax
import jax.numpy as jnp
from jax import lax
from jax.experimental import pallas as pl
from jax.experimental.pallas import tpu as pltpu
from jax.sharding import Mesh
from jax.sharding import PartitionSpec as P

HEAD = 128
BLK = ("blk_y", "blk_z", "blk_c")
NEG = -2.0e38
STAT_ROWS = 16
F32 = jnp.float32
BF16 = jnp.bfloat16


def nt_dot(a, b):
    return lax.dot_general(a, b, (((1,), (1,)), ((), ())), preferred_element_type=F32)


def tn_dot(a, b):
    return lax.dot_general(a, b, (((0,), (0,)), ((), ())), preferred_element_type=F32)


def rope_tables(positions):
    fraction = jnp.arange(0, HEAD, 2).astype(F32) / HEAD
    inverse = jnp.exp(-math.log(500000.0) * fraction)
    angles = positions.astype(F32)[:, None] * inverse[None, :]
    cosine, sine = jnp.cos(angles), jnp.sin(angles)
    return jnp.concatenate([cosine, cosine], axis=1), jnp.concatenate([-sine, sine], axis=1)


def qkv_kernel(where_ref, img_ref, prompt_ref, gain_ref, wq_ref, wk_ref, wv_ref, cos_ref, sin_ref,
               q_ref, kv_ref, own_ref, placed_ref):
    width = prompt_ref.shape[1]
    length = prompt_ref.shape[0]
    own_len = own_ref.shape[0]
    rows = img_ref.shape[0]
    slots = img_ref[:, width : width + 1].astype(F32)
    lanes = lax.broadcasted_iota(jnp.int32, (rows, length), 1).astype(F32)
    flags = jnp.where(slots == lanes, 1.0, 0.0).astype(BF16)
    present = tn_dot(flags, img_ref[:, width:])[:, 1:2] > 0.5
    chosen = tn_dot(flags, img_ref[:, :width])
    placed = jnp.where(present, chosen, prompt_ref[...].astype(F32))
    placed_ref[...] = placed
    mean_square = jnp.mean(placed * placed, axis=1, keepdims=True)
    normed = (placed * lax.rsqrt(mean_square + 1e-05) * gain_ref[...]).astype(BF16)
    first = pl.multiple_of(where_ref[0] * own_len, own_len)
    own_ref[...] = placed_ref[pl.ds(first, own_len), :]
    cosine, sine = cos_ref[...], sin_ref[...]

    def rope(v):
        return (v * cosine + pltpu.roll(v, HEAD // 2, 1) * sine).astype(BF16)

    keys = rope(jnp.dot(normed, wk_ref[...], preferred_element_type=F32))
    values = jnp.dot(normed, wv_ref[...], preferred_element_type=F32).astype(BF16)
    for i in range(kv_ref.shape[0]):
        kv_ref[i, :, :HEAD] = keys
        kv_ref[i, :, HEAD:] = values
    queries = jnp.dot(normed, wq_ref[...], preferred_element_type=F32)
    for h in range(wq_ref.shape[1] // HEAD):
        turned = rope(queries[:, h * HEAD : (h + 1) * HEAD])
        for i in range(q_ref.shape[0]):
            q_ref[i, h * HEAD : (h + 1) * HEAD, :] = turned


def attend_kernel(where_ref, q_ref, near_ref, far_ref, o_ref, s_ref):
    y, z, c = where_ref[1], where_ref[2], where_ref[3]
    zq = pl.program_id(0)
    rows = q_ref.shape[1]
    length = near_ref.shape[1]
    heads = rows // length
    queries = q_ref[0]
    scale = 1.0 / math.sqrt(HEAD)

    def raw(i):
        keys = jnp.concatenate([near_ref[i, :, :HEAD], far_ref[i, :, :HEAD]], axis=0)
        return nt_dot(queries, keys) * scale

    def folded(s, op):
        return op(s[:, :HEAD], s[:, HEAD:])

    def first_pass(i, best):
        s = raw(i)
        s_ref[i] = s
        return jnp.maximum(best, folded(s, jnp.maximum))

    best = lax.fori_loop(0, y, first_pass, jnp.full((rows, HEAD), NEG, F32))
    s = raw(y)
    q_pos = (2 * zq + c) * length + lax.rem(
        lax.broadcasted_iota(jnp.int32, s.shape, 0), length
    )
    lane = lax.broadcasted_iota(jnp.int32, s.shape, 1)
    k_core = jnp.where(lane < length, c, 1 - c)
    k_pos = (2 * z + k_core) * length + jnp.where(lane < length, lane, lane - length)
    s = jnp.where(k_pos <= q_pos, s, NEG)
    s_ref[y] = s
    best = jnp.maximum(best, folded(s, jnp.maximum))
    top = jnp.max(best, axis=1, keepdims=True).astype(BF16).astype(F32)

    def second_pass(i, carry):
        total, mixed = carry
        weights = jnp.exp(s_ref[i] - top)
        total = total + folded(weights, jnp.add)
        values = jnp.concatenate([near_ref[i, :, HEAD:], far_ref[i, :, HEAD:]], axis=0)
        mixed = mixed + jnp.dot(weights.astype(BF16), values, preferred_element_type=F32)
        return total, mixed

    zeros = jnp.zeros((rows, HEAD), F32)
    total, mixed = lax.fori_loop(0, y + 1, second_pass, (zeros, zeros))
    total = jnp.sum(total, axis=1, keepdims=True)
    o_ref[0, :rows, :] = mixed.astype(BF16)
    column = lax.broadcasted_iota(jnp.int32, (length, HEAD), 1)
    tile = jnp.zeros((length, HEAD), F32)
    for h in range(heads):
        part = slice(h * length, (h + 1) * length)
        tile = jnp.where(column == h, top[part], tile)
        tile = jnp.where(column == heads + h, total[part], tile)
    stats = tile.T[: 2 * heads]
    tops, totals = stats[:heads], stats[heads:]
    high = totals.astype(BF16)
    rest = totals - high.astype(F32)
    middle = rest.astype(BF16)
    low = (rest - middle.astype(F32)).astype(BF16)
    packed = jnp.concatenate(
        [tops, high.astype(F32), middle.astype(F32), low.astype(F32),
         jnp.zeros((STAT_ROWS - 4 * heads, length), F32)], axis=0
    )
    o_ref[0, rows:, :] = packed.astype(BF16)


def project_kernel(o_ref, w_ref, out_ref, attended_ref):
    parts = o_ref.shape[0]
    rows = o_ref.shape[1] - STAT_ROWS
    length = o_ref.shape[2]
    heads = rows // length

    @pl.when(pl.program_id(0) == 0)
    def _():
        tops, totals = [], []
        for i in range(parts):
            stats = o_ref[i, rows:, :].astype(F32)
            tops.append(stats[:heads])
            totals.append(stats[heads : 2 * heads] + stats[2 * heads : 3 * heads] + stats[3 * heads : 4 * heads])
        best = functools.reduce(jnp.maximum, tops)
        grown = [jnp.exp(t - best) for t in tops]
        whole = sum(g * t for g, t in zip(grown, totals))
        share = [g / whole for g in grown]
        tile = jnp.concatenate(share + [jnp.zeros((HEAD - parts * heads, length), F32)], axis=0).T
        for h in range(heads):
            part = slice(h * length, (h + 1) * length)
            mixed = sum(
                o_ref[i, part, :].astype(F32) * tile[:, i * heads + h : i * heads + h + 1]
                for i in range(parts)
            )
            attended_ref[:, h * HEAD : (h + 1) * HEAD] = mixed.astype(BF16)

    out_ref[...] = nt_dot(attended_ref[...], w_ref[...]).astype(BF16)


def whole_block(shape):
    return pl.BlockSpec(shape, lambda *_: (0,) * len(shape))


def body(prompt, image_rows, image_slots, norm_gain, w_query, key_matrix, value_matrix, w_out):
    block_len, width = prompt.shape[1:]
    n_uly = lax.axis_size("uly")
    n_y, n_z, n_c = (lax.axis_size(a) for a in BLK)
    own_len = block_len // n_uly
    q_width = w_query.shape[1]
    heads = q_width // HEAD
    y, z, c = (lax.axis_index(a) for a in BLK)
    uly = lax.axis_index("uly")
    where = jnp.stack([uly, y, z, c]).astype(jnp.int32)

    slot_column = image_slots.reshape(-1, 1).astype(BF16)
    ones = jnp.ones_like(slot_column)
    pad = jnp.zeros((slot_column.shape[0], HEAD - 2), BF16)
    tagged = jnp.concatenate([image_rows[0, 0], slot_column, ones, pad], axis=1)
    images = lax.all_to_all(
        jnp.broadcast_to(tagged[None], (n_uly, *tagged.shape)), "uly", 0, 0, tiled=True
    ).reshape(-1, width + HEAD)

    w_turned = w_out.T
    w_near = lax.all_to_all(
        jnp.broadcast_to(w_turned[None], (n_z * n_c, *w_turned.shape)), BLK[1:], 0, 0, tiled=True
    ).reshape(-1, q_width)
    w_all = lax.all_gather(w_near, BLK[0], axis=0, tiled=True)

    block = (y * n_z + z) * n_c + c
    cosine, sine = rope_tables(block * block_len + jnp.arange(block_len, dtype=jnp.int32))

    smem = pl.BlockSpec(memory_space=pltpu.SMEM)
    vmem = pl.BlockSpec(memory_space=pltpu.VMEM)
    queries, key_value, own = pl.pallas_call(
        qkv_kernel,
        out_shape=(
            jax.ShapeDtypeStruct((n_z, heads * block_len, HEAD), BF16),
            jax.ShapeDtypeStruct((n_y, block_len, 2 * HEAD), BF16),
            jax.ShapeDtypeStruct((own_len, width), F32),
        ),
        in_specs=[smem] + [vmem] * 8,
        out_specs=[vmem] * 3,
        scratch_shapes=[pltpu.VMEM((block_len, width), F32)],
        compiler_params=pltpu.CompilerParams(vmem_limit_bytes=24 << 20),
        name="qkv",
    )(where, images, prompt[0], norm_gain[None], w_query, key_matrix, value_matrix, cosine, sine)

    near = lax.all_to_all(key_value, BLK[0], 0, 0, tiled=True)
    asked = lax.all_to_all(queries, BLK[1], 0, 0, tiled=True)
    far = lax.ppermute(near, BLK[2], [(i, (i + 1) % n_c) for i in range(n_c)])

    rows = heads * block_len
    partial = pl.pallas_call(
        attend_kernel,
        out_shape=jax.ShapeDtypeStruct((n_z, rows + STAT_ROWS, HEAD), BF16),
        grid=(n_z,),
        in_specs=[
            smem,
            pl.BlockSpec((1, rows, HEAD), lambda i: (i, 0, 0)),
            whole_block(near.shape),
            whole_block(far.shape),
        ],
        out_specs=pl.BlockSpec((1, rows + STAT_ROWS, HEAD), lambda i: (i, 0, 0)),
        scratch_shapes=[pltpu.VMEM((n_y, rows, 2 * block_len), F32)],
        compiler_params=pltpu.CompilerParams(vmem_limit_bytes=24 << 20),
        name="attend",
    )(where, asked, near, far)

    parts = lax.all_to_all(partial, BLK[1], 0, 0, tiled=True)
    chunk = width // 4
    projected = pl.pallas_call(
        project_kernel,
        out_shape=jax.ShapeDtypeStruct((block_len, width), BF16),
        grid=(width // chunk,),
        in_specs=[whole_block(parts.shape), pl.BlockSpec((chunk, q_width), lambda i: (i, 0))],
        out_specs=pl.BlockSpec((block_len, chunk), lambda i: (0, i)),
        scratch_shapes=[pltpu.VMEM((block_len, q_width), BF16)],
        compiler_params=pltpu.CompilerParams(vmem_limit_bytes=24 << 20),
        name="project",
    )(parts, w_all)

    shares = lax.all_to_all(
        projected.reshape(n_uly, own_len, width), "uly", 0, 0, tiled=True
    )
    return (own + shares.astype(F32).sum(axis=0)).astype(BF16)[None]


def solution(mesh):
    split = Mesh(mesh.devices.reshape(mesh.shape["uly"], 8, 4, 2), ("uly", *BLK))
    placed = (
        P(BLK, None, None),
        P("uly", BLK, None, None),
        P("uly", BLK, None),
        P(),
        P(None, "uly"),
        P(None, "uly"),
        P(None, "uly"),
        P("uly", BLK),
    )
    return jax.shard_map(
        body, mesh=split, in_specs=placed, out_specs=P(BLK, "uly", None), check_vma=False
    )
```

```python
import functools
import math

import jax
import jax.numpy as jnp
from jax import lax
from jax.experimental import pallas as pl
from jax.experimental.pallas import tpu as pltpu
from jax.sharding import Mesh
from jax.sharding import PartitionSpec as P

HEAD = 128
BLK = ("blk_y", "blk_z", "blk_c")
NEG = -(2.0**127)
CHUNK = 4
EXP2_SCALE = math.log2(math.e) / math.sqrt(HEAD)
STAT_ROWS = 16
F32 = jnp.float32
BF16 = jnp.bfloat16


def nt_dot(a, b):
    return lax.dot_general(a, b, (((1,), (1,)), ((), ())), preferred_element_type=F32)


def tn_dot(a, b):
    return lax.dot_general(a, b, (((0,), (0,)), ((), ())), preferred_element_type=F32)


def rope_tables(positions):
    fraction = jnp.arange(0, HEAD, 2).astype(F32) / HEAD
    inverse = jnp.exp(-math.log(500000.0) * fraction)
    angles = positions.astype(F32)[:, None] * inverse[None, :]
    cosine, sine = jnp.cos(angles), jnp.sin(angles)
    return jnp.concatenate([cosine, cosine], axis=1), jnp.concatenate([-sine, sine], axis=1)


def qkv_kernel(img_ref, prompt_ref, gain_ref, table_ref, wq_hbm, wk_hbm, wv_hbm,
               q_ref, kv_ref, own_ref, placed_ref, wq_ref, wk_ref, wv_ref, sems):
    copies = [
        pltpu.make_async_copy(source, target, sems.at[i])
        for i, (source, target) in enumerate(
            [(wk_hbm, wk_ref), (wv_hbm, wv_ref), (wq_hbm, wq_ref)]
        )
    ]
    for copy in copies:
        copy.start()
    length, width = prompt_ref.shape
    own_len = own_ref.shape[0]
    rows = img_ref.shape[0]
    slots = img_ref[:, width : width + 1].astype(F32)
    lanes = lax.broadcasted_iota(jnp.int32, (rows, length), 1).astype(F32)
    flags = jnp.where(slots == lanes, 1.0, 0.0).astype(BF16)
    present = tn_dot(flags, img_ref[:, width:])[:, 1:2] > 0.5
    chosen = tn_dot(flags, img_ref[:, :width])
    placed = jnp.where(present, chosen, prompt_ref[...].astype(F32))
    placed_ref[...] = placed
    mean_square = jnp.mean(placed * placed, axis=1, keepdims=True)
    normed = (placed * lax.rsqrt(mean_square + 1e-05) * gain_ref[...]).astype(BF16)
    first = pl.multiple_of(lax.axis_index("uly") * own_len, own_len)
    own_ref[...] = placed_ref[pl.ds(first, own_len), :]
    cosine, sine = table_ref[:, :HEAD], table_ref[:, HEAD:]

    def rope(v):
        return (v * cosine + pltpu.roll(v, HEAD // 2, 1) * sine).astype(BF16)

    copies[0].wait()
    keys = rope(jnp.dot(normed, wk_ref[...], preferred_element_type=F32))
    copies[1].wait()
    values = jnp.dot(normed, wv_ref[...], preferred_element_type=F32).astype(BF16)
    for i in range(kv_ref.shape[0]):
        kv_ref[i, :, :HEAD] = keys
        kv_ref[i, :, HEAD:] = values
    copies[2].wait()
    queries = jnp.dot(normed, wq_ref[...], preferred_element_type=F32)
    for h in range(wq_ref.shape[1] // HEAD):
        q_ref[h * length : (h + 1) * length, :] = rope(queries[:, h * HEAD : (h + 1) * HEAD])


def in_pieces(values, count):
    pieces = []
    for _ in range(count):
        pieces.append(values.astype(BF16).astype(F32))
        values = values - pieces[-1]
    return pieces


def attend_kernel(*refs):
    n_z = len(refs) - 5
    q_refs = refs[:n_z]
    near_ref, far_ref, o_ref, s_ref, all_q_ref = refs[n_z:]
    y, z, c = (lax.axis_index(a) for a in BLK)
    n_y, length = near_ref.shape[:2]
    rows = q_refs[0].shape[0]
    heads = rows // length
    for d in range(n_z):
        all_q_ref[d] = q_refs[d][...]
    chunks = [(ref, i) for ref in (near_ref, far_ref) for i in range(0, n_y, CHUNK)]
    wide = CHUNK * length

    def folded(s, op):
        return functools.reduce(op, [s[:, i : i + HEAD] for i in range(0, s.shape[1], HEAD)])

    def one_block(d, _):
        zq = lax.rem(z + d, n_z)
        queries = all_q_ref[d]
        column = lax.broadcasted_iota(jnp.int32, (length, HEAD), 1)
        ahead = column - lax.broadcasted_iota(jnp.int32, (length, HEAD), 0)
        ahead = jnp.concatenate([ahead] * heads, axis=0)
        best = jnp.full((rows, HEAD), NEG, F32)
        for k, (ref, i) in enumerate(chunks):
            s = nt_dot(queries, ref[i : i + CHUNK, :, :HEAD].reshape(wide, HEAD))
            core = jnp.int32(0) if ref is near_ref else 2 * c - 1
            for j in range(CHUNK):
                room = ((2 * n_z) * (y - i - j) + 2 * (zq - z) + core) * length
                part = jnp.where(ahead <= room, s[:, j * length : (j + 1) * length], NEG)
                s_ref[k, :, j * length : (j + 1) * length] = part
                best = jnp.maximum(best, part)
        top = jnp.max(best, axis=1, keepdims=True)
        shift = top * EXP2_SCALE
        total = jnp.zeros((rows, HEAD), F32)
        mixed = jnp.zeros((rows, HEAD), F32)
        for k, (ref, i) in enumerate(chunks):
            weights = jnp.exp2(s_ref[k] * EXP2_SCALE - shift)
            total = total + folded(weights, jnp.add)
            values = ref[i : i + CHUNK, :, HEAD:].reshape(wide, HEAD)
            mixed = mixed + jnp.dot(weights.astype(BF16), values, preferred_element_type=F32)
        total = jnp.sum(total, axis=1, keepdims=True)
        tile = jnp.zeros((length, HEAD), F32)
        for h in range(heads):
            part = slice(h * length, (h + 1) * length)
            tile = jnp.where(column == h, top[part], tile)
            tile = jnp.where(column == heads + h, total[part], tile)
        stats = tile.T[: 2 * heads]
        tops, totals = stats[:heads], stats[heads:]
        pieces = [*in_pieces(tops, 3), *in_pieces(totals, 2)]
        pieces.append(jnp.zeros((STAT_ROWS - 5 * heads, length), F32))
        o_ref[zq, :rows, :] = (mixed / total).astype(BF16)
        o_ref[zq, rows:, :] = jnp.concatenate(pieces, axis=0).astype(BF16)
        return 0

    lax.fori_loop(0, n_z, one_block, 0)


def project_kernel(o_ref, w_ref, out_ref, attended_ref):
    parts = o_ref.shape[0]
    rows = o_ref.shape[1] - STAT_ROWS
    length = o_ref.shape[2]
    heads = rows // length

    @pl.when(pl.program_id(0) == 0)
    def _():
        tops, totals = [], []
        for i in range(parts):
            stats = o_ref[i, rows:, :].astype(F32)
            pieces = [stats[k * heads : (k + 1) * heads] for k in range(5)]
            tops.append(pieces[0] + pieces[1] + pieces[2])
            totals.append(pieces[3] + pieces[4])
        best = functools.reduce(jnp.maximum, tops)
        grown = [jnp.exp2((t - best) * EXP2_SCALE) for t in tops]
        grown = [g * t for g, t in zip(grown, totals)]
        whole = sum(grown)
        share = [g / whole for g in grown]
        tile = jnp.concatenate(share + [jnp.zeros((HEAD - parts * heads, length), F32)], axis=0).T
        for h in range(heads):
            part = slice(h * length, (h + 1) * length)
            mixed = sum(
                o_ref[i, part, :].astype(F32) * tile[:, i * heads + h : i * heads + h + 1]
                for i in range(parts)
            )
            attended_ref[:, h * HEAD : (h + 1) * HEAD] = mixed.astype(BF16)

    z = lax.axis_index(BLK[1])
    many, n_c, n_z = w_ref.shape[:3]
    w = jnp.concatenate(
        [w_ref[i, c, lax.rem(zz - z + n_z, n_z)] for i in range(many) for zz in range(n_z) for c in range(n_c)],
        axis=0,
    )
    out_ref[...] = nt_dot(attended_ref[...], w).astype(BF16)


def whole_block(shape):
    return pl.BlockSpec(shape, lambda *_: (0,) * len(shape))


def body(prompt, image_rows, image_slots, norm_gain, w_query, key_matrix, value_matrix, w_out):
    block_len, width = prompt.shape[1:]
    n_uly = lax.axis_size("uly")
    n_y, n_z, n_c = (lax.axis_size(a) for a in BLK)
    own_len = block_len // n_uly
    q_width = w_query.shape[1]
    heads = q_width // HEAD
    y, z, c = (lax.axis_index(a) for a in BLK)
    slot_column = image_slots.reshape(-1, 1).astype(BF16)
    ones = jnp.ones_like(slot_column)
    pad = jnp.zeros((slot_column.shape[0], HEAD - 2), BF16)
    tagged = jnp.concatenate([image_rows[0, 0], slot_column, ones, pad], axis=1)
    tagged = jnp.broadcast_to(tagged[None], (n_uly, *tagged.shape))
    tagged, w_turned = lax.optimization_barrier((tagged, w_out.T))
    images = lax.all_to_all(tagged, "uly", 0, 0, tiled=True).reshape(-1, width + HEAD)

    def from_next(array, axis, d):
        n = lax.axis_size(axis)
        return lax.ppermute(array, axis, [((i + d) % n, i) for i in range(n)])

    w_near = jnp.stack([w_turned] + [from_next(w_turned, BLK[1], d) for d in range(1, n_z)])
    block = (y * n_z + z) * n_c + c
    cosine, sine = rope_tables(block * block_len + jnp.arange(block_len, dtype=jnp.int32))
    table = jnp.concatenate([cosine, sine], axis=1)

    images, table, _ = lax.optimization_barrier((images, table, w_near))
    w_all = lax.all_gather(w_near, (BLK[0], BLK[2]), axis=0, tiled=False)
    w_all = w_all.reshape(n_y, n_c, n_z, *w_near.shape[1:])

    vmem = pl.BlockSpec(memory_space=pltpu.VMEM)
    hbm = pl.BlockSpec(memory_space=pl.ANY)
    rows = heads * block_len
    queries, key_value, own = pl.pallas_call(
        qkv_kernel,
        out_shape=(
            jax.ShapeDtypeStruct((rows, HEAD), BF16),
            jax.ShapeDtypeStruct((n_y, block_len, 2 * HEAD), BF16),
            jax.ShapeDtypeStruct((own_len, width), F32),
        ),
        in_specs=[vmem] * 4 + [hbm] * 3,
        out_specs=[vmem] * 3,
        scratch_shapes=[
            pltpu.VMEM((block_len, width), F32),
            pltpu.VMEM(w_query.shape, BF16),
            pltpu.VMEM(key_matrix.shape, BF16),
            pltpu.VMEM(value_matrix.shape, BF16),
            pltpu.SemaphoreType.DMA((3,)),
        ],
        compiler_params=pltpu.CompilerParams(vmem_limit_bytes=60 << 20),
        name="qkv",
    )(images, prompt[0], norm_gain[None], table, w_query, key_matrix, value_matrix)

    near = lax.all_to_all(key_value, BLK[0], 0, 0, tiled=True)
    asked = [queries] + [from_next(queries, BLK[1], d) for d in range(1, n_z)]
    near, *asked = lax.optimization_barrier((near, *asked))
    far = from_next(near, BLK[2], 1)

    partial = pl.pallas_call(
        attend_kernel,
        out_shape=jax.ShapeDtypeStruct((n_z, rows + STAT_ROWS, HEAD), BF16),
        in_specs=[vmem] * (n_z + 2),
        out_specs=vmem,
        scratch_shapes=[
            pltpu.VMEM((n_c * n_y // CHUNK, rows, CHUNK * block_len), F32),
            pltpu.VMEM((n_z, rows, HEAD), BF16),
        ],
        compiler_params=pltpu.CompilerParams(vmem_limit_bytes=24 << 20),
        name="attend",
    )(*asked, near, far)

    parts = lax.all_to_all(partial, BLK[1], 0, 0, tiled=True)
    piece = w_out.shape[1]
    projected = pl.pallas_call(
        project_kernel,
        out_shape=jax.ShapeDtypeStruct((block_len, width), BF16),
        grid=(n_y // 2,),
        in_specs=[
            whole_block(parts.shape),
            pl.BlockSpec((2, n_c, n_z, piece, q_width), lambda i: (i, 0, 0, 0, 0)),
        ],
        out_specs=pl.BlockSpec((block_len, 2 * width // n_y), lambda i: (0, i)),
        scratch_shapes=[pltpu.VMEM((block_len, q_width), BF16)],
        compiler_params=pltpu.CompilerParams(vmem_limit_bytes=60 << 20),
        name="project",
    )(parts, w_all)

    shares = lax.all_to_all(
        projected.reshape(n_uly, own_len, width), "uly", 0, 0, tiled=True
    )
    return (own + shares.astype(F32).sum(axis=0)).astype(BF16)[None]


def solution(mesh):
    split = Mesh(mesh.devices.reshape(mesh.shape["uly"], 8, 4, 2), ("uly", *BLK))
    placed = (
        P(BLK, None, None),
        P("uly", BLK, None, None),
        P("uly", BLK, None),
        P(),
        P(None, "uly"),
        P(None, "uly"),
        P(None, "uly"),
        P("uly", BLK),
    )
    return jax.shard_map(
        body, mesh=split, in_specs=placed, out_specs=P(BLK, "uly", None), check_vma=False
    )
```

```python
import functools
import math

import jax
import jax.numpy as jnp
from jax import lax
from jax.experimental import pallas as pl
from jax.experimental.pallas import tpu as pltpu
from jax.sharding import Mesh
from jax.sharding import PartitionSpec as P

HEAD = 128
BLK = ("blk_y", "blk_z", "blk_c")
NEG = -(2.0**127)
CHUNK = 4
EXP2_SCALE = math.log2(math.e) / math.sqrt(HEAD)
STAT_ROWS = 16
F32 = jnp.float32
BF16 = jnp.bfloat16


def nt_dot(a, b):
    return lax.dot_general(a, b, (((1,), (1,)), ((), ())), preferred_element_type=F32)


def tn_dot(a, b):
    return lax.dot_general(a, b, (((0,), (0,)), ((), ())), preferred_element_type=F32)


def rope_tables(positions):
    fraction = jnp.arange(0, HEAD, 2).astype(F32) / HEAD
    inverse = jnp.exp(-math.log(500000.0) * fraction)
    angles = positions.astype(F32)[:, None] * inverse[None, :]
    cosine, sine = jnp.cos(angles), jnp.sin(angles)
    return jnp.concatenate([cosine, cosine], axis=1), jnp.concatenate([-sine, sine], axis=1)


def rope(v, table_ref):
    return v * table_ref[:, :HEAD] + pltpu.roll(v, HEAD // 2, 1) * table_ref[:, HEAD:]


def kv_kernel(img_ref, prompt_ref, gain_ref, table_ref, w_ref, normed_ref, kv_ref, own_ref, placed_ref):
    length, width = prompt_ref.shape
    own_len = own_ref.shape[0]
    rows = img_ref.shape[0]
    slots = img_ref[:, width : width + 1].astype(F32)
    lanes = lax.broadcasted_iota(jnp.int32, (rows, length), 1).astype(F32)
    flags = jnp.where(slots == lanes, 1.0, 0.0).astype(BF16)
    present = tn_dot(flags, img_ref[:, width:])[:, 1:2] > 0.5
    chosen = tn_dot(flags, img_ref[:, :width])
    placed = jnp.where(present, chosen, prompt_ref[...].astype(F32))
    placed_ref[...] = placed
    mean_square = jnp.mean(placed * placed, axis=1, keepdims=True)
    normed = (placed * lax.rsqrt(mean_square + 1e-05) * gain_ref[...]).astype(BF16)
    normed_ref[...] = normed
    first = pl.multiple_of(lax.axis_index("uly") * own_len, own_len)
    own_ref[...] = placed_ref[pl.ds(first, own_len), :]
    joined = jnp.dot(normed, w_ref[...], preferred_element_type=F32)
    keys = rope(joined[:, :HEAD], table_ref).T.astype(BF16)
    values = joined[:, HEAD:].astype(BF16)
    for i in range(kv_ref.shape[0]):
        kv_ref[i, :, :HEAD] = keys
        kv_ref[i, :, HEAD:] = values


def q_kernel(normed_ref, table_ref, w_ref, q_ref):
    length = normed_ref.shape[0]
    queries = jnp.dot(normed_ref[...], w_ref[...], preferred_element_type=F32)
    for h in range(w_ref.shape[1] // HEAD):
        part = rope(queries[:, h * HEAD : (h + 1) * HEAD], table_ref)
        q_ref[h * length : (h + 1) * length, :] = part.astype(BF16)


def in_pieces(values, count):
    pieces = []
    for _ in range(count):
        pieces.append(values.astype(BF16).astype(F32))
        values = values - pieces[-1]
    return pieces


def attend_kernel(*refs):
    n_z = len(refs) - 5
    q_refs = refs[:n_z]
    near_ref, far_ref, o_ref, s_ref, all_q_ref = refs[n_z:]
    y, z, c = (lax.axis_index(a) for a in BLK)
    n_y, length = near_ref.shape[:2]
    rows = q_refs[0].shape[0]
    heads = rows // length
    for d in range(n_z):
        all_q_ref[d] = q_refs[d][...]
    chunks = [(ref, i) for ref in (near_ref, far_ref) for i in range(0, n_y, CHUNK)]
    wide = CHUNK * length

    def folded(s, op):
        return functools.reduce(op, [s[:, i : i + HEAD] for i in range(0, s.shape[1], HEAD)])

    def one_block(d, _):
        zq = lax.rem(z + d, n_z)
        queries = all_q_ref[d]
        column = lax.broadcasted_iota(jnp.int32, (length, HEAD), 1)
        ahead = column - lax.broadcasted_iota(jnp.int32, (length, HEAD), 0)
        ahead = jnp.concatenate([ahead] * heads, axis=0)
        best = jnp.full((rows, HEAD), NEG, F32)
        for k, (ref, i) in enumerate(chunks):
            keys = jnp.concatenate([ref[i + j, :, :HEAD] for j in range(CHUNK)], axis=1)
            s = jnp.dot(queries, keys, preferred_element_type=F32)
            core = jnp.int32(0) if ref is near_ref else 2 * c - 1
            for j in range(CHUNK):
                room = ((2 * n_z) * (y - i - j) + 2 * (zq - z) + core) * length
                part = jnp.where(ahead <= room, s[:, j * length : (j + 1) * length], NEG)
                s_ref[k, :, j * length : (j + 1) * length] = part
                best = jnp.maximum(best, part)
        top = jnp.max(best, axis=1, keepdims=True)
        shift = top * EXP2_SCALE
        total = jnp.zeros((rows, HEAD), F32)
        mixed = jnp.zeros((rows, HEAD), F32)
        for k, (ref, i) in enumerate(chunks):
            weights = jnp.exp2(s_ref[k] * EXP2_SCALE - shift)
            total = total + folded(weights, jnp.add)
            values = ref[i : i + CHUNK, :, HEAD:].reshape(wide, HEAD)
            mixed = mixed + jnp.dot(weights.astype(BF16), values, preferred_element_type=F32)
        total = jnp.sum(total, axis=1, keepdims=True)
        tile = jnp.zeros((length, HEAD), F32)
        for h in range(heads):
            part = slice(h * length, (h + 1) * length)
            tile = jnp.where(column == h, top[part], tile)
            tile = jnp.where(column == heads + h, total[part], tile)
        stats = tile.T[: 2 * heads]
        tops, totals = stats[:heads], stats[heads:]
        pieces = [*in_pieces(tops, 3), *in_pieces(totals, 2)]
        pieces.append(jnp.zeros((STAT_ROWS - 5 * heads, length), F32))
        o_ref[zq, :rows, :] = (mixed / total).astype(BF16)
        o_ref[zq, rows:, :] = jnp.concatenate(pieces, axis=0).astype(BF16)
        return 0

    lax.fori_loop(0, n_z, one_block, 0)


def project_kernel(o_ref, w_ref, out_ref, attended_ref):
    parts = o_ref.shape[0]
    rows = o_ref.shape[1] - STAT_ROWS
    length = o_ref.shape[2]
    heads = rows // length

    @pl.when(pl.program_id(0) == 0)
    def _():
        tops, totals = [], []
        for i in range(parts):
            stats = o_ref[i, rows:, :].astype(F32)
            pieces = [stats[k * heads : (k + 1) * heads] for k in range(5)]
            tops.append(pieces[0] + pieces[1] + pieces[2])
            totals.append(pieces[3] + pieces[4])
        best = functools.reduce(jnp.maximum, tops)
        grown = [jnp.exp2((t - best) * EXP2_SCALE) for t in tops]
        grown = [g * t for g, t in zip(grown, totals)]
        whole = sum(grown)
        share = [g / whole for g in grown]
        tile = jnp.concatenate(share + [jnp.zeros((HEAD - parts * heads, length), F32)], axis=0).T
        for h in range(heads):
            part = slice(h * length, (h + 1) * length)
            mixed = sum(
                o_ref[i, part, :].astype(F32) * tile[:, i * heads + h : i * heads + h + 1]
                for i in range(parts)
            )
            attended_ref[:, h * HEAD : (h + 1) * HEAD] = mixed.astype(BF16)

    z = lax.axis_index(BLK[1])
    many, n_c, n_z = w_ref.shape[:3]
    w = jnp.concatenate(
        [w_ref[i, c, lax.rem(zz - z + n_z, n_z)] for i in range(many) for zz in range(n_z) for c in range(n_c)],
        axis=0,
    )
    out_ref[...] = nt_dot(attended_ref[...], w).astype(BF16)


def whole_block(shape):
    return pl.BlockSpec(shape, lambda *_: (0,) * len(shape))


def body(prompt, image_rows, image_slots, norm_gain, w_query, key_matrix, value_matrix, w_out):
    block_len, width = prompt.shape[1:]
    n_uly = lax.axis_size("uly")
    n_y, n_z, n_c = (lax.axis_size(a) for a in BLK)
    own_len = block_len // n_uly
    q_width = w_query.shape[1]
    heads = q_width // HEAD
    y, z, c = (lax.axis_index(a) for a in BLK)
    slot_column = image_slots.reshape(-1, 1).astype(BF16)
    ones = jnp.ones_like(slot_column)
    pad = jnp.zeros((slot_column.shape[0], HEAD - 2), BF16)
    tagged = jnp.concatenate([image_rows[0, 0], slot_column, ones, pad], axis=1)
    tagged = jnp.broadcast_to(tagged[None], (n_uly, *tagged.shape))
    images = lax.all_to_all(tagged, "uly", 0, 0, tiled=True).reshape(-1, width + HEAD)

    def from_next(array, axis, d):
        n = lax.axis_size(axis)
        return lax.ppermute(array, axis, [((i + d) % n, i) for i in range(n)])

    block = (y * n_z + z) * n_c + c
    cosine, sine = rope_tables(block * block_len + jnp.arange(block_len, dtype=jnp.int32))
    table = jnp.concatenate([cosine, sine], axis=1)
    w_kv = jnp.concatenate([key_matrix, value_matrix], axis=1)
    vmem = pl.BlockSpec(memory_space=pltpu.VMEM)
    rows = heads * block_len
    normed, key_value, own = pl.pallas_call(
        kv_kernel,
        out_shape=(
            jax.ShapeDtypeStruct((block_len, width), BF16),
            jax.ShapeDtypeStruct((n_y, block_len, 2 * HEAD), BF16),
            jax.ShapeDtypeStruct((own_len, width), F32),
        ),
        in_specs=[vmem] * 5,
        out_specs=[vmem] * 3,
        scratch_shapes=[pltpu.VMEM((block_len, width), F32)],
        compiler_params=pltpu.CompilerParams(vmem_limit_bytes=24 << 20),
        name="kv",
    )(images, prompt[0], norm_gain[None], table, w_kv)
    queries = pl.pallas_call(
        q_kernel,
        out_shape=jax.ShapeDtypeStruct((rows, HEAD), BF16),
        in_specs=[vmem] * 3,
        out_specs=vmem,
        compiler_params=pltpu.CompilerParams(vmem_limit_bytes=24 << 20),
        cost_estimate=pl.CostEstimate(
            flops=2 * block_len * width * q_width, bytes_accessed=2 * width * q_width, transcendentals=0
        ),
        name="q",
    )(normed, table, w_query)

    near = lax.all_to_all(key_value, BLK[0], 0, 0, tiled=True)
    asked = [queries] + [from_next(queries, BLK[1], d) for d in range(1, n_z)]
    _, w_turned = lax.optimization_barrier((key_value, w_out.T))
    w_near = jnp.stack([w_turned] + [from_next(w_turned, BLK[1], d) for d in range(1, n_z)])
    near, w_near, *asked = lax.optimization_barrier((near, w_near, *asked))
    w_all = lax.all_gather(w_near, (BLK[0], BLK[2]), axis=0, tiled=False)
    w_all = w_all.reshape(n_y, n_c, n_z, *w_near.shape[1:])
    far = from_next(near, BLK[2], 1)

    partial = pl.pallas_call(
        attend_kernel,
        out_shape=jax.ShapeDtypeStruct((n_z, rows + STAT_ROWS, HEAD), BF16),
        in_specs=[vmem] * (n_z + 2),
        out_specs=vmem,
        scratch_shapes=[
            pltpu.VMEM((n_c * n_y // CHUNK, rows, CHUNK * block_len), F32),
            pltpu.VMEM((n_z, rows, HEAD), BF16),
        ],
        compiler_params=pltpu.CompilerParams(vmem_limit_bytes=24 << 20),
        name="attend",
    )(*asked, near, far)

    parts = lax.all_to_all(partial, BLK[1], 0, 0, tiled=True)
    piece = w_out.shape[1]
    projected = pl.pallas_call(
        project_kernel,
        out_shape=jax.ShapeDtypeStruct((block_len, width), BF16),
        grid=(n_y // 2,),
        in_specs=[
            whole_block(parts.shape),
            pl.BlockSpec((2, n_c, n_z, piece, q_width), lambda i: (i, 0, 0, 0, 0)),
        ],
        out_specs=pl.BlockSpec((block_len, 2 * width // n_y), lambda i: (0, i)),
        scratch_shapes=[pltpu.VMEM((block_len, q_width), BF16)],
        compiler_params=pltpu.CompilerParams(vmem_limit_bytes=24 << 20),
        name="project",
    )(parts, w_all)

    shares = lax.all_to_all(
        projected.reshape(n_uly, own_len, width), "uly", 0, 0, tiled=True
    )
    return (own + shares.astype(F32).sum(axis=0)).astype(BF16)[None]


def solution(mesh):
    split = Mesh(mesh.devices.reshape(mesh.shape["uly"], 8, 4, 2), ("uly", *BLK))
    placed = (
        P(BLK, None, None),
        P("uly", BLK, None, None),
        P("uly", BLK, None),
        P(),
        P(None, "uly"),
        P(None, "uly"),
        P(None, "uly"),
        P("uly", BLK),
    )
    return jax.shard_map(
        body, mesh=split, in_specs=placed, out_specs=P(BLK, "uly", None), check_vma=False
    )
```

```python
import functools
import math

import jax
import jax.numpy as jnp
from jax import lax
from jax.experimental import pallas as pl
from jax.experimental.pallas import tpu as pltpu
from jax.sharding import Mesh
from jax.sharding import PartitionSpec as P

HEAD = 128
BLK = ("blk_y", "blk_z", "blk_c")
NEG = -(2.0**127)
CHUNK = 4
W_REPEATS = 4
EXP2_SCALE = math.log2(math.e) / math.sqrt(HEAD)
STAT_ROWS = 16
F32 = jnp.float32
BF16 = jnp.bfloat16


def nt_dot(a, b):
    return lax.dot_general(a, b, (((1,), (1,)), ((), ())), preferred_element_type=F32)


def tn_dot(a, b):
    return lax.dot_general(a, b, (((0,), (0,)), ((), ())), preferred_element_type=F32)


def rope_tables(positions):
    fraction = jnp.arange(0, HEAD, 2).astype(F32) / HEAD
    inverse = jnp.exp(-math.log(500000.0) * fraction)
    angles = positions.astype(F32)[:, None] * inverse[None, :]
    cosine, sine = jnp.cos(angles), jnp.sin(angles)
    return jnp.concatenate([cosine, cosine], axis=1), jnp.concatenate([-sine, sine], axis=1)


def rope(v, table_ref):
    return v * table_ref[:, :HEAD] + pltpu.roll(v, HEAD // 2, 1) * table_ref[:, HEAD:]


def kv_kernel(img_ref, prompt_ref, gain_ref, table_ref, w_ref, normed_ref, kv_ref, own_ref, placed_ref):
    length, width = prompt_ref.shape
    own_len = own_ref.shape[0]
    rows = img_ref.shape[0]
    slots = img_ref[:, width : width + 1].astype(F32)
    lanes = lax.broadcasted_iota(jnp.int32, (rows, length), 1).astype(F32)
    flags = jnp.where(slots == lanes, 1.0, 0.0).astype(BF16)
    present = tn_dot(flags, img_ref[:, width:])[:, 1:2] > 0.5
    chosen = tn_dot(flags, img_ref[:, :width])
    placed = jnp.where(present, chosen, prompt_ref[...].astype(F32))
    placed_ref[...] = placed
    mean_square = jnp.mean(placed * placed, axis=1, keepdims=True)
    normed = (placed * lax.rsqrt(mean_square + 1e-05) * gain_ref[...]).astype(BF16)
    normed_ref[...] = normed
    first = pl.multiple_of(lax.axis_index("uly") * own_len, own_len)
    own_ref[...] = placed_ref[pl.ds(first, own_len), :]
    joined = jnp.dot(normed, w_ref[...], preferred_element_type=F32)
    keys = rope(joined[:, :HEAD], table_ref).T.astype(BF16)
    values = joined[:, HEAD:].astype(BF16)
    for i in range(kv_ref.shape[0]):
        kv_ref[i, :, :HEAD] = keys
        kv_ref[i, :, HEAD:] = values


def q_kernel(normed_ref, table_ref, w_ref, q_ref):
    length = normed_ref.shape[0]
    queries = jnp.dot(normed_ref[...], w_ref[...], preferred_element_type=F32)
    for h in range(w_ref.shape[1] // HEAD):
        part = rope(queries[:, h * HEAD : (h + 1) * HEAD], table_ref).astype(BF16)
        for i in range(q_ref.shape[0]):
            q_ref[i, h * length : (h + 1) * length, :] = part


def in_pieces(values, count):
    pieces = []
    for _ in range(count):
        pieces.append(values.astype(BF16).astype(F32))
        values = values - pieces[-1]
    return pieces


def attend_kernel(q_ref, near_ref, far_ref, o_ref, s_ref):
    y, z, c = (lax.axis_index(a) for a in BLK)
    n_y, length = near_ref.shape[:2]
    n_z, rows = q_ref.shape[:2]
    heads = rows // length
    chunks = [(ref, i) for ref in (near_ref, far_ref) for i in range(0, n_y, CHUNK)]
    wide = CHUNK * length

    def folded(s, op):
        return functools.reduce(op, [s[:, i : i + HEAD] for i in range(0, s.shape[1], HEAD)])

    def one_block(zq, _):
        queries = q_ref[zq]
        column = lax.broadcasted_iota(jnp.int32, (length, HEAD), 1)
        ahead = column - lax.broadcasted_iota(jnp.int32, (length, HEAD), 0)
        ahead = jnp.concatenate([ahead] * heads, axis=0)
        best = jnp.full((rows, HEAD), NEG, F32)
        for k, (ref, i) in enumerate(chunks):
            keys = jnp.concatenate([ref[i + j, :, :HEAD] for j in range(CHUNK)], axis=1)
            s = jnp.dot(queries, keys, preferred_element_type=F32)
            core = jnp.int32(0) if ref is near_ref else 2 * c - 1
            for j in range(CHUNK):
                room = ((2 * n_z) * (y - i - j) + 2 * (zq - z) + core) * length
                part = jnp.where(ahead <= room, s[:, j * length : (j + 1) * length], NEG)
                s_ref[k, :, j * length : (j + 1) * length] = part
                best = jnp.maximum(best, part)
        top = jnp.max(best, axis=1, keepdims=True)
        shift = top * EXP2_SCALE
        total = jnp.zeros((rows, HEAD), F32)
        mixed = jnp.zeros((rows, HEAD), F32)
        for k, (ref, i) in enumerate(chunks):
            weights = jnp.exp2(s_ref[k] * EXP2_SCALE - shift)
            total = total + folded(weights, jnp.add)
            values = ref[i : i + CHUNK, :, HEAD:].reshape(wide, HEAD)
            mixed = mixed + jnp.dot(weights.astype(BF16), values, preferred_element_type=F32)
        total = jnp.sum(total, axis=1, keepdims=True)
        tile = jnp.zeros((length, HEAD), F32)
        for h in range(heads):
            part = slice(h * length, (h + 1) * length)
            tile = jnp.where(column == h, top[part], tile)
            tile = jnp.where(column == heads + h, total[part], tile)
        stats = tile.T[: 2 * heads]
        tops, totals = stats[:heads], stats[heads:]
        pieces = [*in_pieces(tops, 3), *in_pieces(totals, 2)]
        pieces.append(jnp.zeros((STAT_ROWS - 5 * heads, length), F32))
        o_ref[zq, :rows, :] = (mixed / total).astype(BF16)
        o_ref[zq, rows:, :] = jnp.concatenate(pieces, axis=0).astype(BF16)
        return 0

    lax.fori_loop(0, n_z, one_block, 0)


def project_kernel(o_ref, w_ref, out_ref, attended_ref):
    parts = o_ref.shape[0]
    rows = o_ref.shape[1] - STAT_ROWS
    length = o_ref.shape[2]
    heads = rows // length

    @pl.when(pl.program_id(0) == 0)
    def _():
        tops, totals = [], []
        for i in range(parts):
            stats = o_ref[i, rows:, :].astype(F32)
            pieces = [stats[k * heads : (k + 1) * heads] for k in range(5)]
            tops.append(pieces[0] + pieces[1] + pieces[2])
            totals.append(pieces[3] + pieces[4])
        best = functools.reduce(jnp.maximum, tops)
        grown = [jnp.exp2((t - best) * EXP2_SCALE) for t in tops]
        grown = [g * t for g, t in zip(grown, totals)]
        whole = sum(grown)
        share = [g / whole for g in grown]
        tile = jnp.concatenate(share + [jnp.zeros((HEAD - parts * heads, length), F32)], axis=0).T
        for h in range(heads):
            part = slice(h * length, (h + 1) * length)
            mixed = sum(
                o_ref[i, part, :].astype(F32) * tile[:, i * heads + h : i * heads + h + 1]
                for i in range(parts)
            )
            attended_ref[:, h * HEAD : (h + 1) * HEAD] = mixed.astype(BF16)

    many, n_c, n_z = w_ref.shape[:3]
    w = jnp.concatenate(
        [w_ref[i, c, z] for i in range(many) for z in range(n_z) for c in range(n_c)], axis=0
    )
    out_ref[...] = nt_dot(attended_ref[...], w).astype(BF16)


def whole_block(shape):
    return pl.BlockSpec(shape, lambda *_: (0,) * len(shape))


def body(prompt, image_rows, image_slots, norm_gain, w_query, key_matrix, value_matrix, w_out):
    block_len, width = prompt.shape[1:]
    n_uly = lax.axis_size("uly")
    n_y, n_z, n_c = (lax.axis_size(a) for a in BLK)
    own_len = block_len // n_uly
    q_width = w_query.shape[1]
    heads = q_width // HEAD
    y, z, c = (lax.axis_index(a) for a in BLK)
    w_turned = w_out.T
    repeated = lax.optimization_barrier(jnp.broadcast_to(w_turned[None], (W_REPEATS, *w_turned.shape)))
    w_near = lax.all_gather(repeated, BLK[1:], axis=0, tiled=False).reshape(n_z, n_c, W_REPEATS, *w_turned.shape)
    w_near = lax.dynamic_slice(
        w_near, (0, c, 0, 0, 0), (n_z, 1, 1, *w_turned.shape)
    ).reshape(n_z, *w_turned.shape)

    slots = image_slots.reshape(-1, 1).astype(BF16)
    tagged = jnp.pad(image_rows[0, 0], ((0, 0), (0, HEAD)))
    lane = lax.broadcasted_iota(jnp.int32, tagged.shape, 1)
    tagged = jnp.where(lane == width, slots, jnp.where(lane == width + 1, jnp.ones_like(slots), tagged))
    images = lax.all_to_all(
        jnp.broadcast_to(tagged[None], (n_uly, *tagged.shape)), "uly", 0, 0, tiled=True
    ).reshape(-1, width + HEAD)

    block = (y * n_z + z) * n_c + c
    cosine, sine = rope_tables(block * block_len + jnp.arange(block_len, dtype=jnp.int32))
    table = jnp.concatenate([cosine, sine], axis=1)
    w_kv = jnp.concatenate([key_matrix, value_matrix], axis=1)
    vmem = pl.BlockSpec(memory_space=pltpu.VMEM)
    rows = heads * block_len
    normed, key_value, own = pl.pallas_call(
        kv_kernel,
        out_shape=(
            jax.ShapeDtypeStruct((block_len, width), BF16),
            jax.ShapeDtypeStruct((n_y, block_len, 2 * HEAD), BF16),
            jax.ShapeDtypeStruct((own_len, width), F32),
        ),
        in_specs=[vmem] * 5,
        out_specs=[vmem] * 3,
        scratch_shapes=[pltpu.VMEM((block_len, width), F32)],
        compiler_params=pltpu.CompilerParams(vmem_limit_bytes=24 << 20),
        name="kv",
    )(images, prompt[0], norm_gain[None], table, w_kv)
    queries = pl.pallas_call(
        q_kernel,
        out_shape=jax.ShapeDtypeStruct((n_z, rows, HEAD), BF16),
        in_specs=[vmem] * 3,
        out_specs=vmem,
        compiler_params=pltpu.CompilerParams(vmem_limit_bytes=24 << 20),
        cost_estimate=pl.CostEstimate(
            flops=2 * block_len * width * q_width, bytes_accessed=2 * width * q_width, transcendentals=0
        ),
        name="q",
    )(normed, table, w_query)

    near = lax.all_to_all(key_value, BLK[0], 0, 0, tiled=True)
    near, queries = lax.optimization_barrier((near, queries))
    w_all = lax.all_gather(w_near, (BLK[0], BLK[2]), axis=0, tiled=False)
    w_all = w_all.reshape(n_y, n_c, n_z, *w_near.shape[1:])
    asked = lax.all_to_all(queries, BLK[1], 0, 0, tiled=True)
    far = lax.ppermute(near, BLK[2], [((i + 1) % n_c, i) for i in range(n_c)])

    partial = pl.pallas_call(
        attend_kernel,
        out_shape=jax.ShapeDtypeStruct((n_z, rows + STAT_ROWS, HEAD), BF16),
        in_specs=[vmem] * 3,
        out_specs=vmem,
        scratch_shapes=[pltpu.VMEM((n_c * n_y // CHUNK, rows, CHUNK * block_len), F32)],
        compiler_params=pltpu.CompilerParams(vmem_limit_bytes=24 << 20),
        name="attend",
    )(asked, near, far)

    parts = lax.all_to_all(partial, BLK[1], 0, 0, tiled=True)
    piece = w_out.shape[1]
    projected = pl.pallas_call(
        project_kernel,
        out_shape=jax.ShapeDtypeStruct((block_len, width), BF16),
        grid=(n_y // 2,),
        in_specs=[
            whole_block(parts.shape),
            pl.BlockSpec((2, n_c, n_z, piece, q_width), lambda i: (i, 0, 0, 0, 0)),
        ],
        out_specs=pl.BlockSpec((block_len, 2 * width // n_y), lambda i: (0, i)),
        scratch_shapes=[pltpu.VMEM((block_len, q_width), BF16)],
        compiler_params=pltpu.CompilerParams(vmem_limit_bytes=24 << 20),
        name="project",
    )(parts, w_all)

    shares = lax.all_to_all(
        projected.reshape(n_uly, own_len, width), "uly", 0, 0, tiled=True
    )
    return (own + shares.astype(F32).sum(axis=0)).astype(BF16)[None]


def solution(mesh):
    split = Mesh(mesh.devices.reshape(mesh.shape["uly"], 8, 4, 2), ("uly", *BLK))
    placed = (
        P(BLK, None, None),
        P("uly", BLK, None, None),
        P("uly", BLK, None),
        P(),
        P(None, "uly"),
        P(None, "uly"),
        P(None, "uly"),
        P("uly", BLK),
    )
    return jax.shard_map(
        body, mesh=split, in_specs=placed, out_specs=P(BLK, "uly", None), check_vma=False
    )
```

```python
import functools
import math

import jax
import jax.numpy as jnp
from jax import lax
from jax.experimental import pallas as pl
from jax.experimental.pallas import tpu as pltpu
from jax.sharding import Mesh
from jax.sharding import PartitionSpec as P

HEAD = 128
BLK = ("blk_y", "blk_z", "blk_c")
NEG = -(2.0**127)
CHUNK = 2
HIDE = 3.0e38
W_REPEATS = 4
EXP2_SCALE = math.log2(math.e) / math.sqrt(HEAD)
STAT_ROWS = 16
F32 = jnp.float32
BF16 = jnp.bfloat16


def nt_dot(a, b):
    return lax.dot_general(a, b, (((1,), (1,)), ((), ())), preferred_element_type=F32)


def tn_dot(a, b):
    return lax.dot_general(a, b, (((0,), (0,)), ((), ())), preferred_element_type=F32)


def rope_tables(positions):
    fraction = jnp.arange(0, HEAD, 2).astype(F32) / HEAD
    inverse = jnp.exp(-math.log(500000.0) * fraction)
    angles = positions.astype(F32)[:, None] * inverse[None, :]
    cosine, sine = jnp.cos(angles), jnp.sin(angles)
    return jnp.concatenate([cosine, cosine], axis=1), jnp.concatenate([-sine, sine], axis=1)


def rope(v, table_ref):
    return v * table_ref[:, :HEAD] + pltpu.roll(v, HEAD // 2, 1) * table_ref[:, HEAD:]


def kv_kernel(img_ref, prompt_ref, gain_ref, table_ref, w_ref, normed_ref, kv_ref, own_ref, placed_ref):
    length, width = prompt_ref.shape
    own_len = own_ref.shape[0]
    rows = img_ref.shape[0]
    slots = img_ref[:, width : width + 1].astype(F32)
    lanes = lax.broadcasted_iota(jnp.int32, (rows, length), 1).astype(F32)
    flags = jnp.where(slots == lanes, 1.0, 0.0).astype(BF16)
    present = tn_dot(flags, img_ref[:, width:])[:, 1:2] > 0.5
    chosen = tn_dot(flags, img_ref[:, :width])
    placed = jnp.where(present, chosen, prompt_ref[...].astype(F32))
    placed_ref[...] = placed
    mean_square = jnp.mean(placed * placed, axis=1, keepdims=True)
    normed = (placed * lax.rsqrt(mean_square + 1e-05) * gain_ref[...]).astype(BF16)
    normed_ref[...] = normed
    first = pl.multiple_of(lax.axis_index("uly") * own_len, own_len)
    own_ref[...] = placed_ref[pl.ds(first, own_len), :]
    joined = jnp.dot(normed, w_ref[...], preferred_element_type=F32)
    keys = rope(joined[:, :HEAD], table_ref).astype(BF16)
    values = joined[:, HEAD:].T.astype(BF16)
    for i in range(kv_ref.shape[0]):
        kv_ref[i, :, :HEAD] = keys
        kv_ref[i, :, HEAD:] = values


def q_kernel(normed_ref, table_ref, w_ref, q_ref):
    length = normed_ref.shape[0]
    queries = jnp.dot(normed_ref[...], w_ref[...], preferred_element_type=F32)
    for h in range(w_ref.shape[1] // HEAD):
        part = rope(queries[:, h * HEAD : (h + 1) * HEAD], table_ref).T.astype(BF16)
        for i in range(q_ref.shape[0]):
            q_ref[i, :, h * length : (h + 1) * length] = part


def in_pieces(values, count):
    pieces = []
    for _ in range(count):
        pieces.append(values.astype(BF16).astype(F32))
        values = values - pieces[-1]
    return pieces


def attend_kernel(q_ref, near_ref, far_ref, o_ref, s_ref):
    y, z, c = (lax.axis_index(a) for a in BLK)
    n_y, length = near_ref.shape[:2]
    n_z, _, rows = q_ref.shape
    heads = rows // length
    refs = (near_ref, far_ref)
    blocks = [(core, i) for core in range(len(refs)) for i in range(n_y)]
    wide = CHUNK * length

    def folded(s, op):
        return op(s.reshape(-1, 8, rows), axis=0)

    def one_block(zq, _):
        queries = q_ref[zq]
        best = jnp.full((8, rows), NEG, F32)
        for core, ref in enumerate(refs):
            for i in range(0, n_y, CHUNK):
                keys = ref[i : i + CHUNK, :, :HEAD].reshape(wide, HEAD)
                s = jnp.dot(keys, queries, preferred_element_type=F32)
                for j in range(CHUNK):
                    part = s[j * length : (j + 1) * length]
                    s_ref[core, i + j] = part
                    hidden = jnp.where(i + j < y, 0.0, NEG)
                    best = jnp.maximum(best, folded(part, jnp.max) + hidden)
        ahead = lax.broadcasted_iota(jnp.int32, (length, length), 0)
        ahead = ahead - lax.broadcasted_iota(jnp.int32, (length, length), 1)
        ahead = jnp.concatenate([ahead] * heads, axis=1)
        for core in range(len(refs)):
            room = (2 * (zq - z) + core * (2 * c - 1)) * length
            part = jnp.where(ahead <= room, s_ref[core, y], NEG)
            s_ref[core, y] = part
            best = jnp.maximum(best, folded(part, jnp.max))
        top = jnp.max(best, axis=0, keepdims=True)
        shift = top * EXP2_SCALE
        total = jnp.zeros((8, rows), F32)
        mixed = jnp.zeros((HEAD, rows), F32)
        for core, ref in enumerate(refs):
            for i in range(0, n_y, CHUNK):
                weights = []
                for j in range(CHUNK):
                    hidden = jnp.where(i + j <= y, 0.0, HIDE)
                    part = jnp.exp2(s_ref[core, i + j] * EXP2_SCALE - (shift + hidden))
                    total = total + folded(part, jnp.sum)
                    weights.append(part.astype(BF16))
                values = jnp.concatenate([ref[i + j, :, HEAD:] for j in range(CHUNK)], axis=1)
                mixed = mixed + jnp.dot(
                    values, jnp.concatenate(weights, axis=0), preferred_element_type=F32
                )
        total = jnp.sum(total, axis=0, keepdims=True)
        mixed = (mixed * (1.0 / total)).astype(BF16)
        pieces = [*in_pieces(top, 3), *in_pieces(total, 2)]
        across = [slice(h * length, (h + 1) * length) for h in range(heads)]
        for h in range(heads):
            o_ref[zq, h * HEAD : (h + 1) * HEAD, :] = mixed[:, across[h]]
        stats = [piece[:, across[h]] for piece in pieces for h in range(heads)]
        stats.append(jnp.zeros((STAT_ROWS - len(stats), length), F32))
        o_ref[zq, rows:, :] = jnp.concatenate(stats, axis=0).astype(BF16)
        return 0

    lax.fori_loop(0, n_z, one_block, 0)


def project_kernel(o_ref, w_ref, out_ref, attended_ref):
    parts = o_ref.shape[0]
    rows = o_ref.shape[1] - STAT_ROWS
    length = o_ref.shape[2]
    heads = rows // length

    @pl.when(pl.program_id(0) == 0)
    def _():
        tops, totals = [], []
        for i in range(parts):
            stats = o_ref[i, rows:, :].astype(F32)
            pieces = [stats[k * heads : (k + 1) * heads] for k in range(5)]
            tops.append(pieces[0] + pieces[1] + pieces[2])
            totals.append(pieces[3] + pieces[4])
        best = functools.reduce(jnp.maximum, tops)
        grown = [jnp.exp2((t - best) * EXP2_SCALE) for t in tops]
        grown = [g * t for g, t in zip(grown, totals)]
        whole = sum(grown)
        share = [g / whole for g in grown]
        for h in range(heads):
            part = slice(h * HEAD, (h + 1) * HEAD)
            mixed = sum(
                o_ref[i, part, :].astype(F32) * share[i][h : h + 1] for i in range(parts)
            )
            attended_ref[:, part] = mixed.T.astype(BF16)

    many, n_c, n_z = w_ref.shape[:3]
    w = jnp.concatenate(
        [w_ref[i, c, z] for i in range(many) for z in range(n_z) for c in range(n_c)], axis=0
    )
    out_ref[...] = nt_dot(attended_ref[...], w).astype(BF16)


def whole_block(shape):
    return pl.BlockSpec(shape, lambda *_: (0,) * len(shape))


def body(prompt, image_rows, image_slots, norm_gain, w_query, key_matrix, value_matrix, w_out):
    block_len, width = prompt.shape[1:]
    n_uly = lax.axis_size("uly")
    n_y, n_z, n_c = (lax.axis_size(a) for a in BLK)
    own_len = block_len // n_uly
    q_width = w_query.shape[1]
    heads = q_width // HEAD
    y, z, c = (lax.axis_index(a) for a in BLK)
    w_turned = w_out.T
    repeated = lax.optimization_barrier(jnp.broadcast_to(w_turned[None], (W_REPEATS, *w_turned.shape)))
    w_near = lax.all_gather(repeated, BLK[1:], axis=0, tiled=False).reshape(n_z, n_c, W_REPEATS, *w_turned.shape)
    w_near = lax.dynamic_slice(
        w_near, (0, c, 0, 0, 0), (n_z, 1, 1, *w_turned.shape)
    ).reshape(n_z, *w_turned.shape)

    slots = image_slots.reshape(-1, 1).astype(BF16)
    tagged = jnp.pad(image_rows[0, 0], ((0, 0), (0, HEAD)))
    lane = lax.broadcasted_iota(jnp.int32, tagged.shape, 1)
    tagged = jnp.where(lane == width, slots, jnp.where(lane == width + 1, jnp.ones_like(slots), tagged))
    images = lax.all_to_all(
        jnp.broadcast_to(tagged[None], (n_uly, *tagged.shape)), "uly", 0, 0, tiled=True
    ).reshape(-1, width + HEAD)

    block = (y * n_z + z) * n_c + c
    cosine, sine = rope_tables(block * block_len + jnp.arange(block_len, dtype=jnp.int32))
    table = jnp.concatenate([cosine, sine], axis=1)
    w_kv = jnp.concatenate([key_matrix, value_matrix], axis=1)
    vmem = pl.BlockSpec(memory_space=pltpu.VMEM)
    rows = heads * block_len
    normed, key_value, own = pl.pallas_call(
        kv_kernel,
        out_shape=(
            jax.ShapeDtypeStruct((block_len, width), BF16),
            jax.ShapeDtypeStruct((n_y, block_len, 2 * HEAD), BF16),
            jax.ShapeDtypeStruct((own_len, width), F32),
        ),
        in_specs=[vmem] * 5,
        out_specs=[vmem] * 3,
        scratch_shapes=[pltpu.VMEM((block_len, width), F32)],
        compiler_params=pltpu.CompilerParams(vmem_limit_bytes=24 << 20),
        name="kv",
    )(images, prompt[0], norm_gain[None], table, w_kv)
    queries = pl.pallas_call(
        q_kernel,
        out_shape=jax.ShapeDtypeStruct((n_z, HEAD, rows), BF16),
        in_specs=[vmem] * 3,
        out_specs=vmem,
        compiler_params=pltpu.CompilerParams(vmem_limit_bytes=24 << 20),
        cost_estimate=pl.CostEstimate(
            flops=2 * block_len * width * q_width, bytes_accessed=2 * width * q_width, transcendentals=0
        ),
        name="q",
    )(normed, table, w_query)

    near = lax.all_to_all(key_value, BLK[0], 0, 0, tiled=True)
    near, w_near, queries = lax.optimization_barrier((near, w_near, queries))
    w_all = lax.all_gather(w_near, (BLK[0], BLK[2]), axis=0, tiled=False)
    w_all = w_all.reshape(n_y, n_c, n_z, *w_near.shape[1:])
    asked = lax.all_to_all(queries, BLK[1], 0, 0, tiled=True)
    far = lax.ppermute(near, BLK[2], [((i + 1) % n_c, i) for i in range(n_c)])

    partial = pl.pallas_call(
        attend_kernel,
        out_shape=jax.ShapeDtypeStruct((n_z, rows + STAT_ROWS, HEAD), BF16),
        in_specs=[vmem] * 3,
        out_specs=vmem,
        scratch_shapes=[pltpu.VMEM((n_c, n_y, block_len, rows), F32)],
        compiler_params=pltpu.CompilerParams(vmem_limit_bytes=24 << 20),
        name="attend",
    )(asked, near, far)

    parts = lax.all_to_all(partial, BLK[1], 0, 0, tiled=True)
    piece = w_out.shape[1]
    projected = pl.pallas_call(
        project_kernel,
        out_shape=jax.ShapeDtypeStruct((block_len, width), BF16),
        grid=(n_y // 2,),
        in_specs=[
            whole_block(parts.shape),
            pl.BlockSpec((2, n_c, n_z, piece, q_width), lambda i: (i, 0, 0, 0, 0)),
        ],
        out_specs=pl.BlockSpec((block_len, 2 * width // n_y), lambda i: (0, i)),
        scratch_shapes=[pltpu.VMEM((block_len, q_width), BF16)],
        compiler_params=pltpu.CompilerParams(vmem_limit_bytes=24 << 20),
        name="project",
    )(parts, w_all)

    shares = lax.all_to_all(
        projected.reshape(n_uly, own_len, width), "uly", 0, 0, tiled=True
    )
    return (own + shares.astype(F32).sum(axis=0)).astype(BF16)[None]


def solution(mesh):
    split = Mesh(mesh.devices.reshape(mesh.shape["uly"], 8, 4, 2), ("uly", *BLK))
    placed = (
        P(BLK, None, None),
        P("uly", BLK, None, None),
        P("uly", BLK, None),
        P(),
        P(None, "uly"),
        P(None, "uly"),
        P(None, "uly"),
        P("uly", BLK),
    )
    return jax.shard_map(
        body, mesh=split, in_specs=placed, out_specs=P(BLK, "uly", None), check_vma=False
    )
```

```python
import functools
import math

import jax
import jax.numpy as jnp
from jax import lax
from jax.experimental import pallas as pl
from jax.experimental.pallas import tpu as pltpu
from jax.sharding import Mesh
from jax.sharding import PartitionSpec as P

HEAD = 128
BLK = ("blk_y", "blk_z", "blk_c")
NEG = -(2.0**127)
CHUNK = 2
STEPS = 4
HIDE = 3.0e38
W_REPEATS = 4
EXP2_SCALE = math.log2(math.e) / math.sqrt(HEAD)
STAT_ROWS = 16
F32 = jnp.float32
BF16 = jnp.bfloat16


def nt_dot(a, b):
    return lax.dot_general(a, b, (((1,), (1,)), ((), ())), preferred_element_type=F32)


def tn_dot(a, b):
    return lax.dot_general(a, b, (((0,), (0,)), ((), ())), preferred_element_type=F32)


def rope_tables(positions):
    fraction = jnp.arange(0, HEAD, 2).astype(F32) / HEAD
    inverse = jnp.exp(-math.log(500000.0) * fraction)
    angles = positions.astype(F32)[:, None] * inverse[None, :]
    cosine, sine = jnp.cos(angles), jnp.sin(angles)
    return jnp.concatenate([cosine, cosine], axis=1), jnp.concatenate([-sine, sine], axis=1)


def rope(v, table_ref):
    return v * table_ref[:, :HEAD] + pltpu.roll(v, HEAD // 2, 1) * table_ref[:, HEAD:]


def kv_kernel(img_ref, prompt_hbm, gain_ref, table_ref, w_ref, normed_ref, kv_ref, own_ref,
              placed_ref, prompt_ref, sem):
    fetch = pltpu.make_async_copy(prompt_hbm, prompt_ref, sem)
    fetch.start()
    length, width = prompt_ref.shape
    own_len = own_ref.shape[0]
    rows = img_ref.shape[0]
    slots = img_ref[:, width : width + 1].astype(F32)
    lanes = lax.broadcasted_iota(jnp.int32, (rows, length), 1).astype(F32)
    flags = jnp.where(slots == lanes, 1.0, 0.0).astype(BF16)
    present = tn_dot(flags, img_ref[:, width:])[:, 1:2] > 0.5
    chosen = tn_dot(flags, img_ref[:, :width])
    fetch.wait()
    placed = jnp.where(present, chosen, prompt_ref[...].astype(F32))
    placed_ref[...] = placed
    mean_square = jnp.mean(placed * placed, axis=1, keepdims=True)
    normed = (placed * lax.rsqrt(mean_square + 1e-05) * gain_ref[...]).astype(BF16)
    normed_ref[...] = normed
    first = pl.multiple_of(lax.axis_index("uly") * own_len, own_len)
    own_ref[...] = placed_ref[pl.ds(first, own_len), :]
    joined = jnp.dot(normed, w_ref[...], preferred_element_type=F32)
    keys = rope(joined[:, :HEAD], table_ref).astype(BF16)
    values = joined[:, HEAD:].T.astype(BF16)
    for i in range(kv_ref.shape[0]):
        kv_ref[i, :, :HEAD] = keys
        kv_ref[i, :, HEAD:] = values


def q_kernel(normed_ref, table_ref, w_ref, q_ref):
    length = normed_ref.shape[0]
    queries = jnp.dot(normed_ref[...], w_ref[...], preferred_element_type=F32)
    for h in range(w_ref.shape[1] // HEAD):
        part = rope(queries[:, h * HEAD : (h + 1) * HEAD], table_ref).T.astype(BF16)
        for i in range(q_ref.shape[0]):
            q_ref[i, :, h * length : (h + 1) * length] = part


def in_pieces(values, count):
    pieces = []
    for _ in range(count):
        pieces.append(values.astype(BF16).astype(F32))
        values = values - pieces[-1]
    return pieces


def attend_kernel(q_ref, near_ref, far_ref, o_ref, mine_ref, s_ref):
    y, z, c = (lax.axis_index(a) for a in BLK)
    n_y, length = near_ref.shape[:2]
    n_z, _, rows = q_ref.shape
    heads = rows // length
    refs = (near_ref, far_ref)
    blocks = [(core, i) for core in range(len(refs)) for i in range(n_y)]
    wide = CHUNK * length

    def folded(s, op):
        return op(s.reshape(-1, 8, rows), axis=0)

    def one_block(zq, _):
        queries = q_ref[zq]
        best = jnp.full((8, rows), NEG, F32)
        for core, ref in enumerate(refs):
            for i in range(0, n_y, CHUNK):
                keys = ref[i : i + CHUNK, :, :HEAD].reshape(wide, HEAD)
                s = jnp.dot(keys, queries, preferred_element_type=F32)
                for j in range(CHUNK):
                    part = s[j * length : (j + 1) * length]
                    s_ref[core, i + j] = part
                    hidden = jnp.where(i + j < y, 0.0, NEG)
                    best = jnp.maximum(best, folded(part, jnp.max) + hidden)
        ahead = lax.broadcasted_iota(jnp.int32, (length, length), 0)
        ahead = ahead - lax.broadcasted_iota(jnp.int32, (length, length), 1)
        ahead = jnp.concatenate([ahead] * heads, axis=1)
        for core in range(len(refs)):
            room = (2 * (zq - z) + core * (2 * c - 1)) * length
            part = jnp.where(ahead <= room, s_ref[core, y], NEG)
            s_ref[core, y] = part
            best = jnp.maximum(best, folded(part, jnp.max))
        top = jnp.max(best, axis=0, keepdims=True)
        shift = top * EXP2_SCALE
        total = jnp.zeros((8, rows), F32)
        mixed = jnp.zeros((HEAD, rows), F32)
        for core, ref in enumerate(refs):
            for i in range(0, n_y, CHUNK):
                weights = []
                for j in range(CHUNK):
                    hidden = jnp.where(i + j <= y, 0.0, HIDE)
                    part = jnp.exp2(s_ref[core, i + j] * EXP2_SCALE - (shift + hidden))
                    total = total + folded(part, jnp.sum)
                    weights.append(part.astype(BF16))
                values = jnp.concatenate([ref[i + j, :, HEAD:] for j in range(CHUNK)], axis=1)
                mixed = mixed + jnp.dot(
                    values, jnp.concatenate(weights, axis=0), preferred_element_type=F32
                )
        total = jnp.sum(total, axis=0, keepdims=True)
        mixed = mixed * (1.0 / total)
        pieces = [*in_pieces(top, 3), *in_pieces(total, 2)]
        across = [slice(h * length, (h + 1) * length) for h in range(heads)]
        for h in range(heads):
            o_ref[zq, h * HEAD : (h + 1) * HEAD, :] = mixed[:, across[h]].astype(BF16)

        @pl.when(zq == z)
        def _():
            for h in range(heads):
                mine_ref[h * HEAD : (h + 1) * HEAD, :] = mixed[:, across[h]]

        stats = [piece[:, across[h]] for piece in pieces for h in range(heads)]
        stats.append(jnp.zeros((STAT_ROWS - len(stats), length), F32))
        o_ref[zq, rows:, :] = jnp.concatenate(stats, axis=0).astype(BF16)
        return 0

    lax.fori_loop(0, n_z, one_block, 0)


def project_kernel(o_ref, mine_ref, w_hbm, out_ref, attended_ref, w_ref, sems):
    n_y, n_c, n_z, piece = w_ref.shape[:4]
    half = n_y // STEPS
    fetches = [
        pltpu.make_async_copy(w_hbm.at[pl.ds(i * half, half)], w_ref.at[pl.ds(i * half, half)], sems.at[i])
        for i in range(STEPS)
    ]
    for fetch in fetches:
        fetch.start()
    own = lax.axis_index(BLK[1])
    rows = o_ref.shape[1] - STAT_ROWS
    length = o_ref.shape[2]
    heads = rows // length
    tops, totals = [], []
    for i in range(n_z):
        stats = o_ref[i, rows:, :].astype(F32)
        pieces = [stats[k * heads : (k + 1) * heads] for k in range(5)]
        tops.append(pieces[0] + pieces[1] + pieces[2])
        totals.append(pieces[3] + pieces[4])
    best = functools.reduce(jnp.maximum, tops)
    grown = [jnp.exp2((t - best) * EXP2_SCALE) * total for t, total in zip(tops, totals)]
    whole = sum(grown)
    share = [g / whole for g in grown]
    for h in range(heads):
        part = slice(h * HEAD, (h + 1) * HEAD)
        mixed = sum(
            jnp.where(own == i, mine_ref[part, :], o_ref[i, part, :].astype(F32)) * share[i][h : h + 1]
            for i in range(n_z)
        )
        attended_ref[:, part] = mixed.T.astype(BF16)
    columns = half * n_z * n_c * piece
    for i, fetch in enumerate(fetches):
        fetch.wait()
        w = jnp.concatenate(
            [
                w_ref[i * half + j, c, z]
                for j in range(half)
                for z in range(n_z)
                for c in range(n_c)
            ],
            axis=0,
        )
        out_ref[:, i * columns : (i + 1) * columns] = nt_dot(attended_ref[...], w).astype(BF16)


def body(prompt, image_rows, image_slots, norm_gain, w_query, key_matrix, value_matrix, w_out):
    block_len, width = prompt.shape[1:]
    n_uly = lax.axis_size("uly")
    n_y, n_z, n_c = (lax.axis_size(a) for a in BLK)
    own_len = block_len // n_uly
    q_width = w_query.shape[1]
    heads = q_width // HEAD
    y, z, c = (lax.axis_index(a) for a in BLK)
    w_turned = w_out.T
    repeated = lax.optimization_barrier(jnp.broadcast_to(w_turned[None], (W_REPEATS, *w_turned.shape)))
    w_near = lax.all_gather(repeated, BLK[1:], axis=0, tiled=False).reshape(n_z, n_c, W_REPEATS, *w_turned.shape)
    w_near = lax.dynamic_slice(
        w_near, (0, c, 0, 0, 0), (n_z, 1, 1, *w_turned.shape)
    ).reshape(n_z, *w_turned.shape)

    slots = image_slots.reshape(-1, 1).astype(BF16)
    tagged = jnp.pad(image_rows[0, 0], ((0, 0), (0, HEAD)))
    lane = lax.broadcasted_iota(jnp.int32, tagged.shape, 1)
    tagged = jnp.where(lane == width, slots, jnp.where(lane == width + 1, jnp.ones_like(slots), tagged))
    images = lax.all_to_all(
        jnp.broadcast_to(tagged[None], (n_uly, *tagged.shape)), "uly", 0, 0, tiled=True
    ).reshape(-1, width + HEAD)

    block = (y * n_z + z) * n_c + c
    cosine, sine = rope_tables(block * block_len + jnp.arange(block_len, dtype=jnp.int32))
    table = jnp.concatenate([cosine, sine], axis=1)
    w_kv = jnp.concatenate([key_matrix, value_matrix], axis=1)
    vmem = pl.BlockSpec(memory_space=pltpu.VMEM)
    hbm = pl.BlockSpec(memory_space=pltpu.HBM)
    rows = heads * block_len
    normed, key_value, own = pl.pallas_call(
        kv_kernel,
        out_shape=(
            jax.ShapeDtypeStruct((block_len, width), BF16),
            jax.ShapeDtypeStruct((n_y, block_len, 2 * HEAD), BF16),
            jax.ShapeDtypeStruct((own_len, width), F32),
        ),
        in_specs=[vmem, hbm, vmem, vmem, vmem],
        out_specs=[vmem] * 3,
        scratch_shapes=[
            pltpu.VMEM((block_len, width), F32),
            pltpu.VMEM((block_len, width), BF16),
            pltpu.SemaphoreType.DMA,
        ],
        compiler_params=pltpu.CompilerParams(vmem_limit_bytes=24 << 20),
        name="kv",
    )(images, pltpu.with_memory_space_constraint(prompt[0], pltpu.HBM), norm_gain[None], table, w_kv)
    queries = pl.pallas_call(
        q_kernel,
        out_shape=jax.ShapeDtypeStruct((n_z, HEAD, rows), BF16),
        in_specs=[vmem] * 3,
        out_specs=vmem,
        compiler_params=pltpu.CompilerParams(vmem_limit_bytes=24 << 20),
        cost_estimate=pl.CostEstimate(
            flops=2 * block_len * width * q_width, bytes_accessed=2 * width * q_width, transcendentals=0
        ),
        name="q",
    )(normed, table, w_query)

    near = lax.all_to_all(key_value, BLK[0], 0, 0, tiled=True)
    near, w_near, queries = lax.optimization_barrier((near, w_near, queries))
    w_all = lax.all_gather(w_near, (BLK[0], BLK[2]), axis=0, tiled=False)
    w_all = w_all.reshape(n_y, n_c, n_z, *w_near.shape[1:])
    asked = lax.all_to_all(queries, BLK[1], 0, 0, tiled=True)
    far = lax.ppermute(near, BLK[2], [((i + 1) % n_c, i) for i in range(n_c)])

    partial, mine = pl.pallas_call(
        attend_kernel,
        out_shape=(
            jax.ShapeDtypeStruct((n_z, rows + STAT_ROWS, HEAD), BF16),
            jax.ShapeDtypeStruct((rows, HEAD), F32),
        ),
        in_specs=[vmem] * 3,
        out_specs=[vmem] * 2,
        scratch_shapes=[pltpu.VMEM((n_c, n_y, block_len, rows), F32)],
        compiler_params=pltpu.CompilerParams(vmem_limit_bytes=24 << 20),
        name="attend",
    )(asked, near, far)

    parts = lax.all_to_all(partial, BLK[1], 0, 0, tiled=True)
    projected = pl.pallas_call(
        project_kernel,
        out_shape=jax.ShapeDtypeStruct((block_len, width), BF16),
        in_specs=[vmem, vmem, hbm],
        out_specs=vmem,
        scratch_shapes=[
            pltpu.VMEM((block_len, q_width), BF16),
            pltpu.VMEM(w_all.shape, BF16),
            pltpu.SemaphoreType.DMA((STEPS,)),
        ],
        compiler_params=pltpu.CompilerParams(vmem_limit_bytes=24 << 20),
        name="project",
    )(parts, mine, pltpu.with_memory_space_constraint(w_all, pltpu.HBM))

    shares = lax.all_to_all(
        projected.reshape(n_uly, own_len, width), "uly", 0, 0, tiled=True
    )
    return (own + shares.astype(F32).sum(axis=0)).astype(BF16)[None]


def solution(mesh):
    split = Mesh(mesh.devices.reshape(mesh.shape["uly"], 8, 4, 2), ("uly", *BLK))
    placed = (
        P(BLK, None, None),
        P("uly", BLK, None, None),
        P("uly", BLK, None),
        P(),
        P(None, "uly"),
        P(None, "uly"),
        P(None, "uly"),
        P("uly", BLK),
    )
    return jax.shard_map(
        body, mesh=split, in_specs=placed, out_specs=P(BLK, "uly", None), check_vma=False
    )
```

```python
import functools
import math

import jax
import jax.numpy as jnp
from jax import lax
from jax.experimental import pallas as pl
from jax.experimental.pallas import tpu as pltpu
from jax.sharding import Mesh
from jax.sharding import PartitionSpec as P

HEAD = 128
BLK = ("blk_y", "blk_z", "blk_c")
NEG = -(2.0**127)
CHUNK = 2
STEPS = 4
HIDE = float("inf")
W_REPEATS = 4
EXP2_SCALE = math.log2(math.e) / math.sqrt(HEAD)
STAT_ROWS = 16
F32 = jnp.float32
BF16 = jnp.bfloat16


def nt_dot(a, b):
    return lax.dot_general(a, b, (((1,), (1,)), ((), ())), preferred_element_type=F32)


def tn_dot(a, b):
    return lax.dot_general(a, b, (((0,), (0,)), ((), ())), preferred_element_type=F32)


def rope_tables(positions):
    fraction = jnp.arange(0, HEAD, 2).astype(F32) / HEAD
    inverse = jnp.exp(-math.log(500000.0) * fraction)
    angles = positions.astype(F32)[:, None] * inverse[None, :]
    cosine, sine = jnp.cos(angles), jnp.sin(angles)
    return jnp.concatenate([cosine, cosine], axis=1), jnp.concatenate([-sine, sine], axis=1)


def rope(v, table_ref):
    return v * table_ref[:, :HEAD] + pltpu.roll(v, HEAD // 2, 1) * table_ref[:, HEAD:]


def kv_kernel(img_ref, prompt_hbm, gain_ref, table_ref, w_ref, normed_ref, kv_ref, own_ref,
              placed_ref, prompt_ref, sem):
    fetch = pltpu.make_async_copy(prompt_hbm, prompt_ref, sem)
    fetch.start()
    length, width = prompt_ref.shape
    own_len = own_ref.shape[0]
    rows = img_ref.shape[0]
    slots = img_ref[:, width : width + 1].astype(F32)
    lanes = lax.broadcasted_iota(jnp.int32, (rows, length), 1).astype(F32)
    flags = jnp.where(slots == lanes, 1.0, 0.0).astype(BF16)
    present = tn_dot(flags, img_ref[:, width:])[:, 1:2] > 0.5
    chosen = tn_dot(flags, img_ref[:, :width])
    fetch.wait()
    placed = jnp.where(present, chosen, prompt_ref[...].astype(F32))
    placed_ref[...] = placed
    mean_square = jnp.mean(placed * placed, axis=1, keepdims=True)
    normed = (placed * lax.rsqrt(mean_square + 1e-05) * gain_ref[...]).astype(BF16)
    normed_ref[...] = normed
    first = pl.multiple_of(lax.axis_index("uly") * own_len, own_len)
    own_ref[...] = placed_ref[pl.ds(first, own_len), :]
    joined = jnp.dot(normed, w_ref[...], preferred_element_type=F32)
    keys = rope(joined[:, :HEAD], table_ref).astype(BF16)
    values = joined[:, HEAD:].T.astype(BF16)
    for i in range(kv_ref.shape[0]):
        kv_ref[i, :, :HEAD] = keys
        kv_ref[i, :, HEAD:] = values


def q_kernel(normed_ref, table_ref, w_ref, q_ref):
    length = normed_ref.shape[0]
    queries = jnp.dot(normed_ref[...], w_ref[...], preferred_element_type=F32)
    for h in range(w_ref.shape[1] // HEAD):
        part = rope(queries[:, h * HEAD : (h + 1) * HEAD], table_ref).T.astype(BF16)
        for i in range(q_ref.shape[0]):
            q_ref[i, :, h * length : (h + 1) * length] = part


def in_pieces(values, count):
    pieces = []
    for _ in range(count):
        pieces.append(values.astype(BF16).astype(F32))
        values = values - pieces[-1]
    return pieces


def attend_kernel(q_ref, near_ref, far_ref, o_ref, mine_ref, s_ref):
    y, z, c = (lax.axis_index(a) for a in BLK)
    n_y, length = near_ref.shape[:2]
    n_z, _, rows = q_ref.shape
    heads = rows // length
    refs = (near_ref, far_ref)
    blocks = [(core, i) for core in range(len(refs)) for i in range(n_y)]
    wide = CHUNK * length

    def folded(s, op):
        return op(s.reshape(-1, 8, rows), axis=0)

    def one_block(zq, _):
        queries = q_ref[zq]
        best = jnp.full((8, rows), NEG, F32)
        for core, ref in enumerate(refs):
            for i in range(0, n_y, CHUNK):
                keys = ref[i : i + CHUNK, :, :HEAD].reshape(wide, HEAD)
                s = jnp.dot(keys, queries, preferred_element_type=F32)
                for j in range(CHUNK):
                    part = s[j * length : (j + 1) * length]
                    s_ref[core, i + j] = part
                    hidden = jnp.where(i + j < y, 0.0, NEG)
                    best = jnp.maximum(best, folded(part, jnp.max) + hidden)
        ahead = lax.broadcasted_iota(jnp.int32, (length, length), 0)
        ahead = ahead - lax.broadcasted_iota(jnp.int32, (length, length), 1)
        ahead = jnp.concatenate([ahead] * heads, axis=1)
        for core in range(len(refs)):
            room = (2 * (zq - z) + core * (2 * c - 1)) * length
            part = jnp.where(ahead <= room, s_ref[core, y], NEG)
            s_ref[core, y] = part
            best = jnp.maximum(best, folded(part, jnp.max))
        top = jnp.max(best, axis=0, keepdims=True)
        shift = top * EXP2_SCALE
        total = jnp.zeros((8, rows), F32)
        mixed = jnp.zeros((HEAD, rows), F32)
        for core, ref in enumerate(refs):
            for i in range(0, n_y, CHUNK):
                weights = []
                for j in range(CHUNK):
                    hidden = jnp.where(i + j <= y, 0.0, HIDE)
                    part = jnp.exp2(s_ref[core, i + j] * EXP2_SCALE - (shift + hidden))
                    total = total + folded(part, jnp.sum)
                    weights.append(part.astype(BF16))
                values = jnp.concatenate([ref[i + j, :, HEAD:] for j in range(CHUNK)], axis=1)
                mixed = mixed + jnp.dot(
                    values, jnp.concatenate(weights, axis=0), preferred_element_type=F32
                )
        total = jnp.sum(total, axis=0, keepdims=True)
        mixed = mixed * (1.0 / total)
        pieces = [*in_pieces(top, 3), *in_pieces(total, 2)]
        across = [slice(h * length, (h + 1) * length) for h in range(heads)]
        for h in range(heads):
            o_ref[zq, h * HEAD : (h + 1) * HEAD, :] = mixed[:, across[h]].astype(BF16)

        @pl.when(zq == z)
        def _():
            for h in range(heads):
                mine_ref[h * HEAD : (h + 1) * HEAD, :] = mixed[:, across[h]]

        stats = [piece[:, across[h]] for piece in pieces for h in range(heads)]
        stats.append(jnp.zeros((STAT_ROWS - len(stats), length), F32))
        o_ref[zq, rows:, :] = jnp.concatenate(stats, axis=0).astype(BF16)
        return 0

    lax.fori_loop(0, n_z, one_block, 0)


def project_kernel(o_ref, mine_ref, w_hbm, out_ref, attended_ref, w_ref, sems):
    n_c, n_y, n_z, piece = w_ref.shape[:4]
    half = n_y // STEPS
    fetches = [
        pltpu.make_async_copy(w_hbm.at[:, pl.ds(i * half, half)], w_ref.at[:, pl.ds(i * half, half)], sems.at[i])
        for i in range(STEPS)
    ]
    for fetch in fetches:
        fetch.start()
    own = lax.axis_index(BLK[1])
    rows = o_ref.shape[1] - STAT_ROWS
    length = o_ref.shape[2]
    heads = rows // length
    tops, totals = [], []
    for i in range(n_z):
        stats = o_ref[i, rows:, :].astype(F32)
        pieces = [stats[k * heads : (k + 1) * heads] for k in range(5)]
        tops.append(pieces[0] + pieces[1] + pieces[2])
        totals.append(pieces[3] + pieces[4])
    best = functools.reduce(jnp.maximum, tops)
    grown = [jnp.exp2((t - best) * EXP2_SCALE) * total for t, total in zip(tops, totals)]
    whole = sum(grown)
    share = [g / whole for g in grown]
    for h in range(heads):
        part = slice(h * HEAD, (h + 1) * HEAD)
        mixed = sum(
            jnp.where(own == i, mine_ref[part, :], o_ref[i, part, :].astype(F32)) * share[i][h : h + 1]
            for i in range(n_z)
        )
        attended_ref[:, part] = mixed.T.astype(BF16)
    columns = half * n_z * n_c * piece
    for i, fetch in enumerate(fetches):
        fetch.wait()
        w = jnp.concatenate(
            [
                w_ref[c, i * half + j, z]
                for j in range(half)
                for z in range(n_z)
                for c in range(n_c)
            ],
            axis=0,
        )
        out_ref[:, i * columns : (i + 1) * columns] = nt_dot(attended_ref[...], w).astype(BF16)


def body(prompt, image_rows, image_slots, norm_gain, w_query, key_matrix, value_matrix, w_out):
    block_len, width = prompt.shape[1:]
    n_uly = lax.axis_size("uly")
    n_y, n_z, n_c = (lax.axis_size(a) for a in BLK)
    own_len = block_len // n_uly
    q_width = w_query.shape[1]
    heads = q_width // HEAD
    y, z, c = (lax.axis_index(a) for a in BLK)
    w_turned = w_out.T
    repeated = lax.optimization_barrier(jnp.broadcast_to(w_turned[None], (W_REPEATS, *w_turned.shape)))
    w_near = lax.all_gather(repeated, BLK[1:], axis=0, tiled=False).reshape(n_z, n_c, W_REPEATS, *w_turned.shape)
    w_near = lax.dynamic_slice(
        w_near, (0, c, 0, 0, 0), (n_z, 1, 1, *w_turned.shape)
    ).reshape(n_z, *w_turned.shape)

    slots = image_slots.reshape(-1, 1).astype(BF16)
    tagged = jnp.pad(image_rows[0, 0], ((0, 0), (0, HEAD)))
    lane = lax.broadcasted_iota(jnp.int32, tagged.shape, 1)
    tagged = jnp.where(lane == width, slots, jnp.where(lane == width + 1, jnp.ones_like(slots), tagged))
    images = lax.all_to_all(
        jnp.broadcast_to(tagged[None], (n_uly, *tagged.shape)), "uly", 0, 0, tiled=True
    ).reshape(-1, width + HEAD)

    block = (y * n_z + z) * n_c + c
    cosine, sine = rope_tables(block * block_len + jnp.arange(block_len, dtype=jnp.int32))
    table = jnp.concatenate([cosine, sine], axis=1)
    w_kv = jnp.concatenate([key_matrix, value_matrix], axis=1)
    vmem = pl.BlockSpec(memory_space=pltpu.VMEM)
    hbm = pl.BlockSpec(memory_space=pltpu.HBM)
    rows = heads * block_len
    normed, key_value, own = pl.pallas_call(
        kv_kernel,
        out_shape=(
            jax.ShapeDtypeStruct((block_len, width), BF16),
            jax.ShapeDtypeStruct((n_y, block_len, 2 * HEAD), BF16),
            jax.ShapeDtypeStruct((own_len, width), F32),
        ),
        in_specs=[vmem, hbm, vmem, vmem, vmem],
        out_specs=[vmem] * 3,
        scratch_shapes=[
            pltpu.VMEM((block_len, width), F32),
            pltpu.VMEM((block_len, width), BF16),
            pltpu.SemaphoreType.DMA,
        ],
        compiler_params=pltpu.CompilerParams(vmem_limit_bytes=24 << 20),
        name="kv",
    )(images, pltpu.with_memory_space_constraint(prompt[0], pltpu.HBM), norm_gain[None], table, w_kv)
    queries = pl.pallas_call(
        q_kernel,
        out_shape=jax.ShapeDtypeStruct((n_z, HEAD, rows), BF16),
        in_specs=[vmem] * 3,
        out_specs=vmem,
        compiler_params=pltpu.CompilerParams(vmem_limit_bytes=24 << 20),
        cost_estimate=pl.CostEstimate(
            flops=2 * block_len * width * q_width, bytes_accessed=2 * width * q_width, transcendentals=0
        ),
        name="q",
    )(normed, table, w_query)

    near = lax.all_to_all(key_value, BLK[0], 0, 0, tiled=True)
    near, w_near, queries = lax.optimization_barrier((near, w_near, queries))
    w_all = lax.all_gather(w_near, (BLK[2], BLK[0]), axis=0, tiled=False)
    w_all = w_all.reshape(n_c, n_y, n_z, *w_near.shape[1:])
    asked = lax.all_to_all(queries, BLK[1], 0, 0, tiled=True)
    far = lax.ppermute(near, BLK[2], [((i + 1) % n_c, i) for i in range(n_c)])

    partial, mine = pl.pallas_call(
        attend_kernel,
        out_shape=(
            jax.ShapeDtypeStruct((n_z, rows + STAT_ROWS, HEAD), BF16),
            jax.ShapeDtypeStruct((rows, HEAD), F32),
        ),
        in_specs=[vmem] * 3,
        out_specs=[vmem] * 2,
        scratch_shapes=[pltpu.VMEM((n_c, n_y, block_len, rows), F32)],
        compiler_params=pltpu.CompilerParams(vmem_limit_bytes=24 << 20),
        name="attend",
    )(asked, near, far)

    parts = lax.all_to_all(partial, BLK[1], 0, 0, tiled=True)
    projected = pl.pallas_call(
        project_kernel,
        out_shape=jax.ShapeDtypeStruct((block_len, width), BF16),
        in_specs=[vmem, vmem, hbm],
        out_specs=vmem,
        scratch_shapes=[
            pltpu.VMEM((block_len, q_width), BF16),
            pltpu.VMEM(w_all.shape, BF16),
            pltpu.SemaphoreType.DMA((STEPS,)),
        ],
        compiler_params=pltpu.CompilerParams(vmem_limit_bytes=24 << 20),
        name="project",
    )(parts, mine, pltpu.with_memory_space_constraint(w_all, pltpu.HBM))

    shares = lax.all_to_all(
        projected.reshape(n_uly, own_len, width), "uly", 0, 0, tiled=True
    )
    return (own + shares.astype(F32).sum(axis=0)).astype(BF16)[None]


def solution(mesh):
    split = Mesh(mesh.devices.reshape(mesh.shape["uly"], 8, 4, 2), ("uly", *BLK))
    placed = (
        P(BLK, None, None),
        P("uly", BLK, None, None),
        P("uly", BLK, None),
        P(),
        P(None, "uly"),
        P(None, "uly"),
        P(None, "uly"),
        P("uly", BLK),
    )
    return jax.shard_map(
        body, mesh=split, in_specs=placed, out_specs=P(BLK, "uly", None), check_vma=False
    )
```

```python
import functools
import math

import jax
import jax.numpy as jnp
from jax import lax
from jax.experimental import pallas as pl
from jax.experimental.pallas import tpu as pltpu
from jax.sharding import Mesh
from jax.sharding import PartitionSpec as P

HEAD = 128
BLK = ("blk_y", "blk_z", "blk_c")
NEG = -(2.0**127)
CHUNK = 2
STEPS = 4
HIDE = 3.0e38
W_REPEATS = 4
EXP2_SCALE = math.log2(math.e) / math.sqrt(HEAD)
STAT_ROWS = 16
F32 = jnp.float32
BF16 = jnp.bfloat16


def nt_dot(a, b):
    return lax.dot_general(a, b, (((1,), (1,)), ((), ())), preferred_element_type=F32)


def tn_dot(a, b):
    return lax.dot_general(a, b, (((0,), (0,)), ((), ())), preferred_element_type=F32)


def rope_tables(positions):
    fraction = jnp.arange(0, HEAD, 2).astype(F32) / HEAD
    inverse = jnp.exp(-math.log(500000.0) * fraction)
    angles = positions.astype(F32)[:, None] * inverse[None, :]
    cosine, sine = jnp.cos(angles), jnp.sin(angles)
    return jnp.concatenate([cosine, cosine], axis=1), jnp.concatenate([-sine, sine], axis=1)


def tag_kernel(img_ref, slot_ref, out_ref):
    count, width = img_ref.shape
    row = lax.broadcasted_iota(jnp.int32, (count, count), 0)
    own = row == lax.broadcasted_iota(jnp.int32, (count, count), 1)
    slots = jnp.where(own, slot_ref[...].astype(F32), 0.0).sum(axis=1, keepdims=True)
    lane = lax.broadcasted_iota(jnp.int32, (count, HEAD), 1)
    tags = jnp.where(lane == 0, slots, jnp.where(lane == 1, 1.0, 0.0)).astype(BF16)
    for i in range(out_ref.shape[0]):
        out_ref[i, :, :width] = img_ref[...]
        out_ref[i, :, width:] = tags


def rope(v, table_ref):
    return v * table_ref[:, :HEAD] + pltpu.roll(v, HEAD // 2, 1) * table_ref[:, HEAD:]


def kv_kernel(img_ref, prompt_hbm, gain_ref, table_ref, w_ref, normed_ref, kv_ref, own_ref,
              placed_ref, prompt_ref, sem):
    fetch = pltpu.make_async_copy(prompt_hbm, prompt_ref, sem)
    fetch.start()
    length, width = prompt_ref.shape
    own_len = own_ref.shape[0]
    rows = img_ref.shape[0]
    slots = img_ref[:, width : width + 1].astype(F32)
    lanes = lax.broadcasted_iota(jnp.int32, (rows, length), 1).astype(F32)
    flags = jnp.where(slots == lanes, 1.0, 0.0).astype(BF16)
    present = tn_dot(flags, img_ref[:, width:])[:, 1:2] > 0.5
    chosen = tn_dot(flags, img_ref[:, :width])
    fetch.wait()
    placed = jnp.where(present, chosen, prompt_ref[...].astype(F32))
    placed_ref[...] = placed
    mean_square = jnp.mean(placed * placed, axis=1, keepdims=True)
    normed = (placed * lax.rsqrt(mean_square + 1e-05) * gain_ref[...]).astype(BF16)
    normed_ref[...] = normed
    first = pl.multiple_of(lax.axis_index("uly") * own_len, own_len)
    own_ref[...] = placed_ref[pl.ds(first, own_len), :]
    joined = jnp.dot(normed, w_ref[...], preferred_element_type=F32)
    keys = rope(joined[:, :HEAD], table_ref).astype(BF16)
    values = joined[:, HEAD:].T.astype(BF16)
    for i in range(kv_ref.shape[0]):
        kv_ref[i, :, :HEAD] = keys
        kv_ref[i, :, HEAD:] = values


def q_kernel(normed_ref, table_ref, w_ref, q_ref):
    length = normed_ref.shape[0]
    queries = jnp.dot(normed_ref[...], w_ref[...], preferred_element_type=F32)
    for h in range(w_ref.shape[1] // HEAD):
        part = rope(queries[:, h * HEAD : (h + 1) * HEAD], table_ref).T.astype(BF16)
        for i in range(q_ref.shape[0]):
            q_ref[i, :, h * length : (h + 1) * length] = part


def in_pieces(values, count):
    pieces = []
    for _ in range(count):
        pieces.append(values.astype(BF16).astype(F32))
        values = values - pieces[-1]
    return pieces


def attend_kernel(q_ref, near_ref, far_ref, o_ref, mine_ref, s_ref):
    y, z, c = (lax.axis_index(a) for a in BLK)
    n_y, length = near_ref.shape[:2]
    n_z, _, rows = q_ref.shape
    heads = rows // length
    refs = (near_ref, far_ref)
    blocks = [(core, i) for core in range(len(refs)) for i in range(n_y)]
    wide = CHUNK * length

    def folded(s, op):
        return op(s.reshape(-1, 8, rows), axis=0)

    def one_block(zq, _):
        queries = q_ref[zq]
        best = jnp.full((8, rows), NEG, F32)
        for core, ref in enumerate(refs):
            for i in range(0, n_y, CHUNK):
                keys = ref[i : i + CHUNK, :, :HEAD].reshape(wide, HEAD)
                s = jnp.dot(keys, queries, preferred_element_type=F32)
                for j in range(CHUNK):
                    part = s[j * length : (j + 1) * length]
                    s_ref[core, i + j] = part
                    hidden = jnp.where(i + j < y, 0.0, NEG)
                    best = jnp.maximum(best, folded(part, jnp.max) + hidden)
        ahead = lax.broadcasted_iota(jnp.int32, (length, length), 0)
        ahead = ahead - lax.broadcasted_iota(jnp.int32, (length, length), 1)
        ahead = jnp.concatenate([ahead] * heads, axis=1)
        for core in range(len(refs)):
            room = (2 * (zq - z) + core * (2 * c - 1)) * length
            part = jnp.where(ahead <= room, s_ref[core, y], NEG)
            s_ref[core, y] = part
            best = jnp.maximum(best, folded(part, jnp.max))
        top = jnp.max(best, axis=0, keepdims=True)
        shift = top * EXP2_SCALE
        total = jnp.zeros((8, rows), F32)
        mixed = jnp.zeros((HEAD, rows), F32)
        for core, ref in enumerate(refs):
            for i in range(0, n_y, CHUNK):
                weights = []
                for j in range(CHUNK):
                    hidden = jnp.where(i + j <= y, 0.0, HIDE)
                    part = jnp.exp2(s_ref[core, i + j] * EXP2_SCALE - (shift + hidden))
                    total = total + folded(part, jnp.sum)
                    weights.append(part.astype(BF16))
                values = jnp.concatenate([ref[i + j, :, HEAD:] for j in range(CHUNK)], axis=1)
                mixed = mixed + jnp.dot(
                    values, jnp.concatenate(weights, axis=0), preferred_element_type=F32
                )
        total = jnp.sum(total, axis=0, keepdims=True)
        mixed = mixed * (1.0 / total)
        pieces = [*in_pieces(top, 3), *in_pieces(total, 2)]
        across = [slice(h * length, (h + 1) * length) for h in range(heads)]
        for h in range(heads):
            o_ref[zq, h * HEAD : (h + 1) * HEAD, :] = mixed[:, across[h]].astype(BF16)

        @pl.when(zq == z)
        def _():
            for h in range(heads):
                mine_ref[h * HEAD : (h + 1) * HEAD, :] = mixed[:, across[h]]

        stats = [piece[:, across[h]] for piece in pieces for h in range(heads)]
        stats.append(jnp.zeros((STAT_ROWS - len(stats), length), F32))
        o_ref[zq, rows:, :] = jnp.concatenate(stats, axis=0).astype(BF16)
        return 0

    lax.fori_loop(0, n_z, one_block, 0)


def project_kernel(o_ref, mine_ref, w_hbm, out_ref, attended_ref, w_ref, sems):
    n_y, n_c, n_z, piece = w_ref.shape[:4]
    half = n_y // STEPS
    fetches = [
        pltpu.make_async_copy(w_hbm.at[pl.ds(i * half, half)], w_ref.at[pl.ds(i * half, half)], sems.at[i])
        for i in range(STEPS)
    ]
    for fetch in fetches:
        fetch.start()
    own = lax.axis_index(BLK[1])
    rows = o_ref.shape[1] - STAT_ROWS
    length = o_ref.shape[2]
    heads = rows // length
    tops, totals = [], []
    for i in range(n_z):
        stats = o_ref[i, rows:, :].astype(F32)
        pieces = [stats[k * heads : (k + 1) * heads] for k in range(5)]
        tops.append(pieces[0] + pieces[1] + pieces[2])
        totals.append(pieces[3] + pieces[4])
    best = functools.reduce(jnp.maximum, tops)
    grown = [jnp.exp2((t - best) * EXP2_SCALE) * total for t, total in zip(tops, totals)]
    whole = sum(grown)
    share = [g / whole for g in grown]
    for h in range(heads):
        part = slice(h * HEAD, (h + 1) * HEAD)
        mixed = sum(
            jnp.where(own == i, mine_ref[part, :], o_ref[i, part, :].astype(F32)) * share[i][h : h + 1]
            for i in range(n_z)
        )
        attended_ref[:, part] = mixed.T.astype(BF16)
    columns = half * n_z * n_c * piece
    for i, fetch in enumerate(fetches):
        fetch.wait()
        w = jnp.concatenate(
            [
                w_ref[i * half + j, c, z]
                for j in range(half)
                for z in range(n_z)
                for c in range(n_c)
            ],
            axis=0,
        )
        out_ref[:, i * columns : (i + 1) * columns] = nt_dot(attended_ref[...], w).astype(BF16)


def body(prompt, image_rows, image_slots, norm_gain, w_query, key_matrix, value_matrix, w_out):
    block_len, width = prompt.shape[1:]
    n_uly = lax.axis_size("uly")
    n_y, n_z, n_c = (lax.axis_size(a) for a in BLK)
    own_len = block_len // n_uly
    q_width = w_query.shape[1]
    heads = q_width // HEAD
    y, z, c = (lax.axis_index(a) for a in BLK)
    w_turned = w_out.T
    repeated = lax.optimization_barrier(jnp.broadcast_to(w_turned[None], (W_REPEATS, *w_turned.shape)))
    w_near = lax.all_gather(repeated, BLK[1:], axis=0, tiled=False).reshape(n_z, n_c, W_REPEATS, *w_turned.shape)
    w_near = lax.dynamic_slice(
        w_near, (0, c, 0, 0, 0), (n_z, 1, 1, *w_turned.shape)
    ).reshape(n_z, *w_turned.shape)

    vmem = pl.BlockSpec(memory_space=pltpu.VMEM)
    tagged = pl.pallas_call(
        tag_kernel,
        out_shape=jax.ShapeDtypeStruct((n_uly, image_rows.shape[2], width + HEAD), BF16),
        in_specs=[vmem] * 2,
        out_specs=vmem,
        compiler_params=pltpu.CompilerParams(vmem_limit_bytes=60 << 20),
        name="tag",
    )(image_rows[0, 0], image_slots[0])
    images = lax.all_to_all(tagged, "uly", 0, 0, tiled=True).reshape(-1, width + HEAD)

    block = (y * n_z + z) * n_c + c
    cosine, sine = rope_tables(block * block_len + jnp.arange(block_len, dtype=jnp.int32))
    table = jnp.concatenate([cosine, sine], axis=1)
    w_kv = jnp.concatenate([key_matrix, value_matrix], axis=1)
    hbm = pl.BlockSpec(memory_space=pltpu.HBM)
    rows = heads * block_len
    normed, key_value, own = pl.pallas_call(
        kv_kernel,
        out_shape=(
            jax.ShapeDtypeStruct((block_len, width), BF16),
            jax.ShapeDtypeStruct((n_y, block_len, 2 * HEAD), BF16),
            jax.ShapeDtypeStruct((own_len, width), F32),
        ),
        in_specs=[vmem, hbm, vmem, vmem, vmem],
        out_specs=[vmem] * 3,
        scratch_shapes=[
            pltpu.VMEM((block_len, width), F32),
            pltpu.VMEM((block_len, width), BF16),
            pltpu.SemaphoreType.DMA,
        ],
        compiler_params=pltpu.CompilerParams(vmem_limit_bytes=24 << 20),
        name="kv",
    )(images, pltpu.with_memory_space_constraint(prompt[0], pltpu.HBM), norm_gain[None], table, w_kv)
    queries = pl.pallas_call(
        q_kernel,
        out_shape=jax.ShapeDtypeStruct((n_z, HEAD, rows), BF16),
        in_specs=[vmem] * 3,
        out_specs=vmem,
        compiler_params=pltpu.CompilerParams(vmem_limit_bytes=24 << 20),
        cost_estimate=pl.CostEstimate(
            flops=2 * block_len * width * q_width, bytes_accessed=2 * width * q_width, transcendentals=0
        ),
        name="q",
    )(normed, table, w_query)

    near = lax.all_to_all(key_value, BLK[0], 0, 0, tiled=True)
    near, w_near, queries = lax.optimization_barrier((near, w_near, queries))
    w_all = lax.all_gather(w_near, (BLK[0], BLK[2]), axis=0, tiled=False)
    w_all = w_all.reshape(n_y, n_c, n_z, *w_near.shape[1:])
    asked = lax.all_to_all(queries, BLK[1], 0, 0, tiled=True)
    far = lax.ppermute(near, BLK[2], [((i + 1) % n_c, i) for i in range(n_c)])

    partial, mine = pl.pallas_call(
        attend_kernel,
        out_shape=(
            jax.ShapeDtypeStruct((n_z, rows + STAT_ROWS, HEAD), BF16),
            jax.ShapeDtypeStruct((rows, HEAD), F32),
        ),
        in_specs=[vmem] * 3,
        out_specs=[vmem] * 2,
        scratch_shapes=[pltpu.VMEM((n_c, n_y, block_len, rows), F32)],
        compiler_params=pltpu.CompilerParams(vmem_limit_bytes=24 << 20),
        name="attend",
    )(asked, near, far)

    parts = lax.all_to_all(partial, BLK[1], 0, 0, tiled=True)
    projected = pl.pallas_call(
        project_kernel,
        out_shape=jax.ShapeDtypeStruct((block_len, width), BF16),
        in_specs=[vmem, vmem, hbm],
        out_specs=vmem,
        scratch_shapes=[
            pltpu.VMEM((block_len, q_width), BF16),
            pltpu.VMEM(w_all.shape, BF16),
            pltpu.SemaphoreType.DMA((STEPS,)),
        ],
        compiler_params=pltpu.CompilerParams(vmem_limit_bytes=24 << 20),
        name="project",
    )(parts, mine, pltpu.with_memory_space_constraint(w_all, pltpu.HBM))

    shares = lax.all_to_all(
        projected.reshape(n_uly, own_len, width), "uly", 0, 0, tiled=True
    )
    return (own + shares.astype(F32).sum(axis=0)).astype(BF16)[None]


def solution(mesh):
    split = Mesh(mesh.devices.reshape(mesh.shape["uly"], 8, 4, 2), ("uly", *BLK))
    placed = (
        P(BLK, None, None),
        P("uly", BLK, None, None),
        P("uly", BLK, None),
        P(),
        P(None, "uly"),
        P(None, "uly"),
        P(None, "uly"),
        P("uly", BLK),
    )
    return jax.shard_map(
        body, mesh=split, in_specs=placed, out_specs=P(BLK, "uly", None), check_vma=False
    )
```

```python
import functools
import math

import jax
import jax.numpy as jnp
from jax import lax
from jax.experimental import pallas as pl
from jax.experimental.pallas import tpu as pltpu
from jax.sharding import Mesh
from jax.sharding import PartitionSpec as P

HEAD = 128
BLK = ("blk_y", "blk_z", "blk_c")
NEG = -(2.0**127)
CHUNK = 2
STEPS = 4
HIDE = 3.0e38
W_REPEATS = 4
EXP2_SCALE = math.log2(math.e) / math.sqrt(HEAD)
STAT_ROWS = 16
F32 = jnp.float32
BF16 = jnp.bfloat16


def nt_dot(a, b):
    return lax.dot_general(a, b, (((1,), (1,)), ((), ())), preferred_element_type=F32)


def tn_dot(a, b):
    return lax.dot_general(a, b, (((0,), (0,)), ((), ())), preferred_element_type=F32)


def rope_tables(positions):
    fraction = jnp.arange(0, HEAD, 2).astype(F32) / HEAD
    inverse = jnp.exp(-math.log(500000.0) * fraction)
    angles = positions.astype(F32)[:, None] * inverse[None, :]
    cosine, sine = jnp.cos(angles), jnp.sin(angles)
    return jnp.concatenate([cosine, cosine], axis=1), jnp.concatenate([-sine, sine], axis=1)


def tag_kernel(img_ref, slot_ref, w_ref, out_ref, again_ref):
    for i in range(again_ref.shape[0]):
        again_ref[i] = w_ref[...]
    count, width = img_ref.shape
    row = lax.broadcasted_iota(jnp.int32, (count, count), 0)
    own = row == lax.broadcasted_iota(jnp.int32, (count, count), 1)
    slots = jnp.where(own, slot_ref[...].astype(F32), 0.0).sum(axis=1, keepdims=True)
    lane = lax.broadcasted_iota(jnp.int32, (count, HEAD), 1)
    tags = jnp.where(lane == 0, slots, jnp.where(lane == 1, 1.0, 0.0)).astype(BF16)
    for i in range(out_ref.shape[0]):
        out_ref[i, :, :width] = img_ref[...]
        out_ref[i, :, width:] = tags


def rope(v, table_ref):
    return v * table_ref[:, :HEAD] + pltpu.roll(v, HEAD // 2, 1) * table_ref[:, HEAD:]


def kv_kernel(img_ref, prompt_hbm, gain_ref, table_ref, w_ref, normed_ref, kv_ref, own_ref,
              placed_ref, prompt_ref, sem):
    fetch = pltpu.make_async_copy(prompt_hbm, prompt_ref, sem)
    fetch.start()
    length, width = prompt_ref.shape
    own_len = own_ref.shape[0]
    rows = img_ref.shape[0]
    slots = img_ref[:, width : width + 1].astype(F32)
    lanes = lax.broadcasted_iota(jnp.int32, (rows, length), 1).astype(F32)
    flags = jnp.where(slots == lanes, 1.0, 0.0).astype(BF16)
    present = tn_dot(flags, img_ref[:, width:])[:, 1:2] > 0.5
    chosen = tn_dot(flags, img_ref[:, :width])
    fetch.wait()
    placed = jnp.where(present, chosen, prompt_ref[...].astype(F32))
    placed_ref[...] = placed
    mean_square = jnp.mean(placed * placed, axis=1, keepdims=True)
    normed = (placed * lax.rsqrt(mean_square + 1e-05) * gain_ref[...]).astype(BF16)
    normed_ref[...] = normed
    first = pl.multiple_of(lax.axis_index("uly") * own_len, own_len)
    own_ref[...] = placed_ref[pl.ds(first, own_len), :]
    joined = jnp.dot(normed, w_ref[...], preferred_element_type=F32)
    keys = rope(joined[:, :HEAD], table_ref).astype(BF16)
    values = joined[:, HEAD:].T.astype(BF16)
    for i in range(kv_ref.shape[0]):
        kv_ref[i, :, :HEAD] = keys
        kv_ref[i, :, HEAD:] = values


def q_kernel(normed_ref, table_ref, w_ref, q_ref):
    length = normed_ref.shape[0]
    queries = jnp.dot(normed_ref[...], w_ref[...], preferred_element_type=F32)
    for h in range(w_ref.shape[1] // HEAD):
        part = rope(queries[:, h * HEAD : (h + 1) * HEAD], table_ref).T.astype(BF16)
        for i in range(q_ref.shape[0]):
            q_ref[i, :, h * length : (h + 1) * length] = part


def in_pieces(values, count):
    pieces = []
    for _ in range(count):
        pieces.append(values.astype(BF16).astype(F32))
        values = values - pieces[-1]
    return pieces


def attend_kernel(q_ref, near_ref, far_ref, o_ref, mine_ref, s_ref):
    y, z, c = (lax.axis_index(a) for a in BLK)
    n_y, length = near_ref.shape[:2]
    n_z, _, rows = q_ref.shape
    heads = rows // length
    refs = (near_ref, far_ref)
    blocks = [(core, i) for core in range(len(refs)) for i in range(n_y)]
    wide = CHUNK * length

    def folded(s, op):
        return op(s.reshape(-1, 8, rows), axis=0)

    def one_block(zq, _):
        queries = q_ref[zq]
        best = jnp.full((8, rows), NEG, F32)
        for core, ref in enumerate(refs):
            for i in range(0, n_y, CHUNK):
                keys = ref[i : i + CHUNK, :, :HEAD].reshape(wide, HEAD)
                s = jnp.dot(keys, queries, preferred_element_type=F32)
                for j in range(CHUNK):
                    part = s[j * length : (j + 1) * length]
                    s_ref[core, i + j] = part
                    hidden = jnp.where(i + j < y, 0.0, NEG)
                    best = jnp.maximum(best, folded(part, jnp.max) + hidden)
        ahead = lax.broadcasted_iota(jnp.int32, (length, length), 0)
        ahead = ahead - lax.broadcasted_iota(jnp.int32, (length, length), 1)
        ahead = jnp.concatenate([ahead] * heads, axis=1)
        for core in range(len(refs)):
            room = (2 * (zq - z) + core * (2 * c - 1)) * length
            part = jnp.where(ahead <= room, s_ref[core, y], NEG)
            s_ref[core, y] = part
            best = jnp.maximum(best, folded(part, jnp.max))
        top = jnp.max(best, axis=0, keepdims=True)
        shift = top * EXP2_SCALE
        total = jnp.zeros((8, rows), F32)
        mixed = jnp.zeros((HEAD, rows), F32)
        for core, ref in enumerate(refs):
            for i in range(0, n_y, CHUNK):
                weights = []
                for j in range(CHUNK):
                    hidden = jnp.where(i + j <= y, 0.0, HIDE)
                    part = jnp.exp2(s_ref[core, i + j] * EXP2_SCALE - (shift + hidden))
                    total = total + folded(part, jnp.sum)
                    weights.append(part.astype(BF16))
                values = jnp.concatenate([ref[i + j, :, HEAD:] for j in range(CHUNK)], axis=1)
                mixed = mixed + jnp.dot(
                    values, jnp.concatenate(weights, axis=0), preferred_element_type=F32
                )
        total = jnp.sum(total, axis=0, keepdims=True)
        mixed = mixed * (1.0 / total)
        pieces = [*in_pieces(top, 3), *in_pieces(total, 2)]
        across = [slice(h * length, (h + 1) * length) for h in range(heads)]
        for h in range(heads):
            o_ref[zq, h * HEAD : (h + 1) * HEAD, :] = mixed[:, across[h]].astype(BF16)

        @pl.when(zq == z)
        def _():
            for h in range(heads):
                mine_ref[h * HEAD : (h + 1) * HEAD, :] = mixed[:, across[h]]

        stats = [piece[:, across[h]] for piece in pieces for h in range(heads)]
        stats.append(jnp.zeros((STAT_ROWS - len(stats), length), F32))
        o_ref[zq, rows:, :] = jnp.concatenate(stats, axis=0).astype(BF16)
        return 0

    lax.fori_loop(0, n_z, one_block, 0)


def project_kernel(o_ref, mine_ref, w_hbm, out_ref, attended_ref, w_ref, sems):
    n_y, n_c, n_z, piece = w_ref.shape[:4]
    half = n_y // STEPS
    fetches = [
        pltpu.make_async_copy(w_hbm.at[pl.ds(i * half, half)], w_ref.at[pl.ds(i * half, half)], sems.at[i])
        for i in range(STEPS)
    ]
    for fetch in fetches:
        fetch.start()
    own = lax.axis_index(BLK[1])
    rows = o_ref.shape[1] - STAT_ROWS
    length = o_ref.shape[2]
    heads = rows // length
    tops, totals = [], []
    for i in range(n_z):
        stats = o_ref[i, rows:, :].astype(F32)
        pieces = [stats[k * heads : (k + 1) * heads] for k in range(5)]
        tops.append(pieces[0] + pieces[1] + pieces[2])
        totals.append(pieces[3] + pieces[4])
    best = functools.reduce(jnp.maximum, tops)
    grown = [jnp.exp2((t - best) * EXP2_SCALE) * total for t, total in zip(tops, totals)]
    whole = sum(grown)
    share = [g / whole for g in grown]
    for h in range(heads):
        part = slice(h * HEAD, (h + 1) * HEAD)
        mixed = sum(
            jnp.where(own == i, mine_ref[part, :], o_ref[i, part, :].astype(F32)) * share[i][h : h + 1]
            for i in range(n_z)
        )
        attended_ref[:, part] = mixed.T.astype(BF16)
    columns = half * n_z * n_c * piece
    for i, fetch in enumerate(fetches):
        fetch.wait()
        w = jnp.concatenate(
            [
                w_ref[i * half + j, c, z]
                for j in range(half)
                for z in range(n_z)
                for c in range(n_c)
            ],
            axis=0,
        )
        out_ref[:, i * columns : (i + 1) * columns] = nt_dot(attended_ref[...], w).astype(BF16)


def body(prompt, image_rows, image_slots, norm_gain, w_query, key_matrix, value_matrix, w_out):
    block_len, width = prompt.shape[1:]
    n_uly = lax.axis_size("uly")
    n_y, n_z, n_c = (lax.axis_size(a) for a in BLK)
    own_len = block_len // n_uly
    q_width = w_query.shape[1]
    heads = q_width // HEAD
    y, z, c = (lax.axis_index(a) for a in BLK)
    w_turned = w_out.T
    vmem = pl.BlockSpec(memory_space=pltpu.VMEM)
    tagged, repeated = pl.pallas_call(
        tag_kernel,
        out_shape=(
            jax.ShapeDtypeStruct((n_uly, image_rows.shape[2], width + HEAD), BF16),
            jax.ShapeDtypeStruct((W_REPEATS, *w_turned.shape), BF16),
        ),
        in_specs=[vmem] * 3,
        out_specs=[vmem] * 2,
        compiler_params=pltpu.CompilerParams(vmem_limit_bytes=60 << 20),
        name="tag",
    )(image_rows[0, 0], image_slots[0], w_turned)
    w_near = lax.all_gather(repeated, BLK[1:], axis=0, tiled=False).reshape(n_z, n_c, W_REPEATS, *w_turned.shape)
    w_near = lax.dynamic_slice(
        w_near, (0, c, 0, 0, 0), (n_z, 1, 1, *w_turned.shape)
    ).reshape(n_z, *w_turned.shape)
    images = lax.all_to_all(tagged, "uly", 0, 0, tiled=True).reshape(-1, width + HEAD)

    block = (y * n_z + z) * n_c + c
    cosine, sine = rope_tables(block * block_len + jnp.arange(block_len, dtype=jnp.int32))
    table = jnp.concatenate([cosine, sine], axis=1)
    w_kv = jnp.concatenate([key_matrix, value_matrix], axis=1)
    hbm = pl.BlockSpec(memory_space=pltpu.HBM)
    rows = heads * block_len
    normed, key_value, own = pl.pallas_call(
        kv_kernel,
        out_shape=(
            jax.ShapeDtypeStruct((block_len, width), BF16),
            jax.ShapeDtypeStruct((n_y, block_len, 2 * HEAD), BF16),
            jax.ShapeDtypeStruct((own_len, width), F32),
        ),
        in_specs=[vmem, hbm, vmem, vmem, vmem],
        out_specs=[vmem] * 3,
        scratch_shapes=[
            pltpu.VMEM((block_len, width), F32),
            pltpu.VMEM((block_len, width), BF16),
            pltpu.SemaphoreType.DMA,
        ],
        compiler_params=pltpu.CompilerParams(vmem_limit_bytes=24 << 20),
        name="kv",
    )(images, pltpu.with_memory_space_constraint(prompt[0], pltpu.HBM), norm_gain[None], table, w_kv)
    queries = pl.pallas_call(
        q_kernel,
        out_shape=jax.ShapeDtypeStruct((n_z, HEAD, rows), BF16),
        in_specs=[vmem] * 3,
        out_specs=vmem,
        compiler_params=pltpu.CompilerParams(vmem_limit_bytes=24 << 20),
        cost_estimate=pl.CostEstimate(
            flops=2 * block_len * width * q_width, bytes_accessed=2 * width * q_width, transcendentals=0
        ),
        name="q",
    )(normed, table, w_query)

    near = lax.all_to_all(key_value, BLK[0], 0, 0, tiled=True)
    near, w_near, queries = lax.optimization_barrier((near, w_near, queries))
    w_all = lax.all_gather(w_near, (BLK[0], BLK[2]), axis=0, tiled=False)
    w_all = w_all.reshape(n_y, n_c, n_z, *w_near.shape[1:])
    asked = lax.all_to_all(queries, BLK[1], 0, 0, tiled=True)
    far = lax.ppermute(near, BLK[2], [((i + 1) % n_c, i) for i in range(n_c)])

    partial, mine = pl.pallas_call(
        attend_kernel,
        out_shape=(
            jax.ShapeDtypeStruct((n_z, rows + STAT_ROWS, HEAD), BF16),
            jax.ShapeDtypeStruct((rows, HEAD), F32),
        ),
        in_specs=[vmem] * 3,
        out_specs=[vmem] * 2,
        scratch_shapes=[pltpu.VMEM((n_c, n_y, block_len, rows), F32)],
        compiler_params=pltpu.CompilerParams(vmem_limit_bytes=24 << 20),
        name="attend",
    )(asked, near, far)

    parts = lax.all_to_all(partial, BLK[1], 0, 0, tiled=True)
    projected = pl.pallas_call(
        project_kernel,
        out_shape=jax.ShapeDtypeStruct((block_len, width), BF16),
        in_specs=[vmem, vmem, hbm],
        out_specs=vmem,
        scratch_shapes=[
            pltpu.VMEM((block_len, q_width), BF16),
            pltpu.VMEM(w_all.shape, BF16),
            pltpu.SemaphoreType.DMA((STEPS,)),
        ],
        compiler_params=pltpu.CompilerParams(vmem_limit_bytes=24 << 20),
        name="project",
    )(parts, mine, pltpu.with_memory_space_constraint(w_all, pltpu.HBM))

    shares = lax.all_to_all(
        projected.reshape(n_uly, own_len, width), "uly", 0, 0, tiled=True
    )
    return (own + shares.astype(F32).sum(axis=0)).astype(BF16)[None]


def solution(mesh):
    split = Mesh(mesh.devices.reshape(mesh.shape["uly"], 8, 4, 2), ("uly", *BLK))
    placed = (
        P(BLK, None, None),
        P("uly", BLK, None, None),
        P("uly", BLK, None),
        P(),
        P(None, "uly"),
        P(None, "uly"),
        P(None, "uly"),
        P("uly", BLK),
    )
    return jax.shard_map(
        body, mesh=split, in_specs=placed, out_specs=P(BLK, "uly", None), check_vma=False
    )
```

```python
import functools
import math

import jax
import jax.numpy as jnp
from jax import lax
from jax.experimental import pallas as pl
from jax.experimental.pallas import tpu as pltpu
from jax.sharding import Mesh
from jax.sharding import PartitionSpec as P

HEAD = 128
BLK = ("blk_y", "blk_z", "blk_c")
NEG = -(2.0**127)
CHUNK = 2
STEPS = 4
HIDE = 3.0e38
REPEATED_ROWS = 176
EXP2_SCALE = math.log2(math.e) / math.sqrt(HEAD)
STAT_ROWS = 16
F32 = jnp.float32
BF16 = jnp.bfloat16


def nt_dot(a, b):
    return lax.dot_general(a, b, (((1,), (1,)), ((), ())), preferred_element_type=F32)


def tn_dot(a, b):
    return lax.dot_general(a, b, (((0,), (0,)), ((), ())), preferred_element_type=F32)


def rope_tables(positions):
    fraction = jnp.arange(0, HEAD, 2).astype(F32) / HEAD
    inverse = jnp.exp(-math.log(500000.0) * fraction)
    angles = positions.astype(F32)[:, None] * inverse[None, :]
    cosine, sine = jnp.cos(angles), jnp.sin(angles)
    return jnp.concatenate([cosine, cosine], axis=1), jnp.concatenate([-sine, sine], axis=1)


def tag_kernel(img_ref, slot_ref, w_ref, out_ref, again_ref):
    piece = w_ref.shape[0]
    for i in range(0, again_ref.shape[0], piece):
        count_here = min(piece, again_ref.shape[0] - i)
        again_ref[i : i + count_here, :] = w_ref[:count_here, :]
    count, width = img_ref.shape
    row = lax.broadcasted_iota(jnp.int32, (count, count), 0)
    own = row == lax.broadcasted_iota(jnp.int32, (count, count), 1)
    slots = jnp.where(own, slot_ref[...].astype(F32), 0.0).sum(axis=1, keepdims=True)
    lane = lax.broadcasted_iota(jnp.int32, (count, HEAD), 1)
    tags = jnp.where(lane == 0, slots, jnp.where(lane == 1, 1.0, 0.0)).astype(BF16)
    for i in range(out_ref.shape[0]):
        out_ref[i, :, :width] = img_ref[...]
        out_ref[i, :, width:] = tags


def rope(v, table_ref):
    return v * table_ref[:, :HEAD] + pltpu.roll(v, HEAD // 2, 1) * table_ref[:, HEAD:]


def kv_kernel(img_ref, prompt_hbm, gain_ref, table_ref, w_ref, normed_ref, kv_ref, own_ref,
              placed_ref, prompt_ref, sem):
    fetch = pltpu.make_async_copy(prompt_hbm, prompt_ref, sem)
    fetch.start()
    length, width = prompt_ref.shape
    own_len = own_ref.shape[0]
    rows = img_ref.shape[0]
    slots = img_ref[:, width : width + 1].astype(F32)
    lanes = lax.broadcasted_iota(jnp.int32, (rows, length), 1).astype(F32)
    flags = jnp.where(slots == lanes, 1.0, 0.0).astype(BF16)
    present = tn_dot(flags, img_ref[:, width:])[:, 1:2] > 0.5
    chosen = tn_dot(flags, img_ref[:, :width])
    fetch.wait()
    placed = jnp.where(present, chosen, prompt_ref[...].astype(F32))
    placed_ref[...] = placed
    mean_square = jnp.mean(placed * placed, axis=1, keepdims=True)
    normed = (placed * lax.rsqrt(mean_square + 1e-05) * gain_ref[...]).astype(BF16)
    normed_ref[...] = normed
    first = pl.multiple_of(lax.axis_index("uly") * own_len, own_len)
    own_ref[...] = placed_ref[pl.ds(first, own_len), :]
    joined = jnp.dot(normed, w_ref[...], preferred_element_type=F32)
    keys = rope(joined[:, :HEAD], table_ref).astype(BF16)
    values = joined[:, HEAD:].T.astype(BF16)
    for i in range(kv_ref.shape[0]):
        kv_ref[i, :, :HEAD] = keys
        kv_ref[i, :, HEAD:] = values


def q_kernel(normed_ref, table_ref, w_ref, q_ref):
    length = normed_ref.shape[0]
    queries = jnp.dot(normed_ref[...], w_ref[...], preferred_element_type=F32)
    for h in range(w_ref.shape[1] // HEAD):
        part = rope(queries[:, h * HEAD : (h + 1) * HEAD], table_ref).T.astype(BF16)
        for i in range(q_ref.shape[0]):
            q_ref[i, :, h * length : (h + 1) * length] = part


def in_pieces(values, count):
    pieces = []
    for _ in range(count):
        pieces.append(values.astype(BF16).astype(F32))
        values = values - pieces[-1]
    return pieces


def attend_kernel(q_ref, near_ref, far_ref, o_ref, mine_ref, s_ref):
    y, z, c = (lax.axis_index(a) for a in BLK)
    n_y, length = near_ref.shape[:2]
    n_z, _, rows = q_ref.shape
    heads = rows // length
    refs = (near_ref, far_ref)
    blocks = [(core, i) for core in range(len(refs)) for i in range(n_y)]
    wide = CHUNK * length

    def folded(s, op):
        return op(s.reshape(-1, 8, rows), axis=0)

    def one_block(zq, _):
        queries = q_ref[zq]
        best = jnp.full((8, rows), NEG, F32)
        for core, ref in enumerate(refs):
            for i in range(0, n_y, CHUNK):
                keys = ref[i : i + CHUNK, :, :HEAD].reshape(wide, HEAD)
                s = jnp.dot(keys, queries, preferred_element_type=F32)
                for j in range(CHUNK):
                    part = s[j * length : (j + 1) * length]
                    s_ref[core, i + j] = part
                    hidden = jnp.where(i + j < y, 0.0, NEG)
                    best = jnp.maximum(best, folded(part, jnp.max) + hidden)
        ahead = lax.broadcasted_iota(jnp.int32, (length, length), 0)
        ahead = ahead - lax.broadcasted_iota(jnp.int32, (length, length), 1)
        ahead = jnp.concatenate([ahead] * heads, axis=1)
        for core in range(len(refs)):
            room = (2 * (zq - z) + core * (2 * c - 1)) * length
            part = jnp.where(ahead <= room, s_ref[core, y], NEG)
            s_ref[core, y] = part
            best = jnp.maximum(best, folded(part, jnp.max))
        top = jnp.max(best, axis=0, keepdims=True)
        shift = top * EXP2_SCALE
        total = jnp.zeros((8, rows), F32)
        mixed = jnp.zeros((HEAD, rows), F32)
        for core, ref in enumerate(refs):
            for i in range(0, n_y, CHUNK):
                weights = []
                for j in range(CHUNK):
                    hidden = jnp.where(i + j <= y, 0.0, HIDE)
                    part = jnp.exp2(s_ref[core, i + j] * EXP2_SCALE - (shift + hidden))
                    total = total + folded(part, jnp.sum)
                    weights.append(part.astype(BF16))
                values = jnp.concatenate([ref[i + j, :, HEAD:] for j in range(CHUNK)], axis=1)
                mixed = mixed + jnp.dot(
                    values, jnp.concatenate(weights, axis=0), preferred_element_type=F32
                )
        total = jnp.sum(total, axis=0, keepdims=True)
        mixed = mixed * (1.0 / total)
        pieces = [*in_pieces(top, 3), *in_pieces(total, 2)]
        across = [slice(h * length, (h + 1) * length) for h in range(heads)]
        for h in range(heads):
            o_ref[zq, h * HEAD : (h + 1) * HEAD, :] = mixed[:, across[h]].astype(BF16)

        @pl.when(zq == z)
        def _():
            for h in range(heads):
                mine_ref[h * HEAD : (h + 1) * HEAD, :] = mixed[:, across[h]]

        stats = [piece[:, across[h]] for piece in pieces for h in range(heads)]
        stats.append(jnp.zeros((STAT_ROWS - len(stats), length), F32))
        o_ref[zq, rows:, :] = jnp.concatenate(stats, axis=0).astype(BF16)
        return 0

    lax.fori_loop(0, n_z, one_block, 0)


def project_kernel(o_ref, mine_ref, w_hbm, out_ref, attended_ref, w_ref, sems):
    n_y, n_c, n_z, piece = w_ref.shape[:4]
    half = n_y // STEPS
    fetches = [
        pltpu.make_async_copy(w_hbm.at[pl.ds(i * half, half)], w_ref.at[pl.ds(i * half, half)], sems.at[i])
        for i in range(STEPS)
    ]
    for fetch in fetches:
        fetch.start()
    own = lax.axis_index(BLK[1])
    rows = o_ref.shape[1] - STAT_ROWS
    length = o_ref.shape[2]
    heads = rows // length
    tops, totals = [], []
    for i in range(n_z):
        stats = o_ref[i, rows:, :].astype(F32)
        pieces = [stats[k * heads : (k + 1) * heads] for k in range(5)]
        tops.append(pieces[0] + pieces[1] + pieces[2])
        totals.append(pieces[3] + pieces[4])
    best = functools.reduce(jnp.maximum, tops)
    grown = [jnp.exp2((t - best) * EXP2_SCALE) * total for t, total in zip(tops, totals)]
    whole = sum(grown)
    share = [g / whole for g in grown]
    for h in range(heads):
        part = slice(h * HEAD, (h + 1) * HEAD)
        mixed = sum(
            jnp.where(own == i, mine_ref[part, :], o_ref[i, part, :].astype(F32)) * share[i][h : h + 1]
            for i in range(n_z)
        )
        attended_ref[:, part] = mixed.T.astype(BF16)
    columns = half * n_z * n_c * piece
    for i, fetch in enumerate(fetches):
        fetch.wait()
        w = jnp.concatenate(
            [
                w_ref[i * half + j, c, z]
                for j in range(half)
                for z in range(n_z)
                for c in range(n_c)
            ],
            axis=0,
        )
        out_ref[:, i * columns : (i + 1) * columns] = nt_dot(attended_ref[...], w).astype(BF16)


def body(prompt, image_rows, image_slots, norm_gain, w_query, key_matrix, value_matrix, w_out):
    block_len, width = prompt.shape[1:]
    n_uly = lax.axis_size("uly")
    n_y, n_z, n_c = (lax.axis_size(a) for a in BLK)
    own_len = block_len // n_uly
    q_width = w_query.shape[1]
    heads = q_width // HEAD
    y, z, c = (lax.axis_index(a) for a in BLK)
    w_turned = w_out.T
    vmem = pl.BlockSpec(memory_space=pltpu.VMEM)
    tagged, repeated = pl.pallas_call(
        tag_kernel,
        out_shape=(
            jax.ShapeDtypeStruct((n_uly, image_rows.shape[2], width + HEAD), BF16),
            jax.ShapeDtypeStruct((REPEATED_ROWS, q_width), BF16),
        ),
        in_specs=[vmem] * 3,
        out_specs=[vmem] * 2,
        compiler_params=pltpu.CompilerParams(vmem_limit_bytes=60 << 20),
        name="tag",
    )(image_rows[0, 0], image_slots[0], w_turned)
    w_near = lax.all_gather(repeated, BLK[1:], axis=0, tiled=False).reshape(n_z, n_c, REPEATED_ROWS, q_width)
    w_near = lax.dynamic_slice(
        w_near, (0, c, 0, 0), (n_z, 1, *w_turned.shape)
    ).reshape(n_z, *w_turned.shape)
    images = lax.all_to_all(tagged, "uly", 0, 0, tiled=True).reshape(-1, width + HEAD)

    block = (y * n_z + z) * n_c + c
    cosine, sine = rope_tables(block * block_len + jnp.arange(block_len, dtype=jnp.int32))
    table = jnp.concatenate([cosine, sine], axis=1)
    w_kv = jnp.concatenate([key_matrix, value_matrix], axis=1)
    hbm = pl.BlockSpec(memory_space=pltpu.HBM)
    rows = heads * block_len
    normed, key_value, own = pl.pallas_call(
        kv_kernel,
        out_shape=(
            jax.ShapeDtypeStruct((block_len, width), BF16),
            jax.ShapeDtypeStruct((n_y, block_len, 2 * HEAD), BF16),
            jax.ShapeDtypeStruct((own_len, width), F32),
        ),
        in_specs=[vmem, hbm, vmem, vmem, vmem],
        out_specs=[vmem] * 3,
        scratch_shapes=[
            pltpu.VMEM((block_len, width), F32),
            pltpu.VMEM((block_len, width), BF16),
            pltpu.SemaphoreType.DMA,
        ],
        compiler_params=pltpu.CompilerParams(vmem_limit_bytes=24 << 20),
        name="kv",
    )(images, pltpu.with_memory_space_constraint(prompt[0], pltpu.HBM), norm_gain[None], table, w_kv)
    queries = pl.pallas_call(
        q_kernel,
        out_shape=jax.ShapeDtypeStruct((n_z, HEAD, rows), BF16),
        in_specs=[vmem] * 3,
        out_specs=vmem,
        compiler_params=pltpu.CompilerParams(vmem_limit_bytes=24 << 20),
        cost_estimate=pl.CostEstimate(
            flops=2 * block_len * width * q_width, bytes_accessed=2 * width * q_width, transcendentals=0
        ),
        name="q",
    )(normed, table, w_query)

    near = lax.all_to_all(key_value, BLK[0], 0, 0, tiled=True)
    near, w_near, queries = lax.optimization_barrier((near, w_near, queries))
    w_all = lax.all_gather(w_near, (BLK[0], BLK[2]), axis=0, tiled=False)
    w_all = w_all.reshape(n_y, n_c, n_z, *w_near.shape[1:])
    asked = lax.all_to_all(queries, BLK[1], 0, 0, tiled=True)
    far = lax.ppermute(near, BLK[2], [((i + 1) % n_c, i) for i in range(n_c)])

    partial, mine = pl.pallas_call(
        attend_kernel,
        out_shape=(
            jax.ShapeDtypeStruct((n_z, rows + STAT_ROWS, HEAD), BF16),
            jax.ShapeDtypeStruct((rows, HEAD), F32),
        ),
        in_specs=[vmem] * 3,
        out_specs=[vmem] * 2,
        scratch_shapes=[pltpu.VMEM((n_c, n_y, block_len, rows), F32)],
        compiler_params=pltpu.CompilerParams(vmem_limit_bytes=24 << 20),
        name="attend",
    )(asked, near, far)

    parts = lax.all_to_all(partial, BLK[1], 0, 0, tiled=True)
    projected = pl.pallas_call(
        project_kernel,
        out_shape=jax.ShapeDtypeStruct((block_len, width), BF16),
        in_specs=[vmem, vmem, hbm],
        out_specs=vmem,
        scratch_shapes=[
            pltpu.VMEM((block_len, q_width), BF16),
            pltpu.VMEM(w_all.shape, BF16),
            pltpu.SemaphoreType.DMA((STEPS,)),
        ],
        compiler_params=pltpu.CompilerParams(vmem_limit_bytes=24 << 20),
        name="project",
    )(parts, mine, pltpu.with_memory_space_constraint(w_all, pltpu.HBM))

    shares = lax.all_to_all(
        projected.reshape(n_uly, own_len, width), "uly", 0, 0, tiled=True
    )
    return (own + shares.astype(F32).sum(axis=0)).astype(BF16)[None]


def solution(mesh):
    split = Mesh(mesh.devices.reshape(mesh.shape["uly"], 8, 4, 2), ("uly", *BLK))
    placed = (
        P(BLK, None, None),
        P("uly", BLK, None, None),
        P("uly", BLK, None),
        P(),
        P(None, "uly"),
        P(None, "uly"),
        P(None, "uly"),
        P("uly", BLK),
    )
    return jax.shard_map(
        body, mesh=split, in_specs=placed, out_specs=P(BLK, "uly", None), check_vma=False
    )
```
